512 devices in a mesh: grp: 16 (over y, x_lo), blk: 32 (over z, x_hi, core).
Axes of the slice: x: 4 (x_hi: 2, x_lo: 2; x = x_hi * 2 + x_lo), y: 8, z: 8, core: 2. Of those that a mesh axis runs over, the one named last changes fastest.
Arguments:
- amplitudes: float32 [128, 128, 2048], P('blk', None, 'grp'), may hold values from -6 to 6
- ladder_ints: float32 [2048, 2048], P('grp', 'blk'), may hold values from -0.375 to 0.375
- cycle_ints: float32 [2048, 2048], P('grp', 'blk'), may hold values from -0.375 to 0.375
- occ_coupling: float32 [128, 128], replicated, may hold values from -1.5 to 1.5
- occ_irrep: int32 [128], replicated, may hold values from 0 to 7
- pair_irrep: int32 [16], replicated, may hold values from 0 to 7
- screen: int32 [16, 16], replicated, may hold values 0 or 1
- block_order: int32 [16], replicated, may hold values from 0 to 15, each once
Outputs:
- residual: float32 [128, 128, 2048], P('blk', None, 'grp')
The draws below stay inside these ranges and needn't reach their ends.
Inputs may be any that keep to these rules, and one draw needn't show every extreme that they name: block_order names every block once.
All inputs are finite; a program needn't handle non-finite values.
Results may differ from the reference program's by a relative error of at most 0.000071.
Values sent between devices are 32-bit elements; how exact they have to be, the bound alone decides.
A program may use at most 64 MiB of HBM per device.

```python
import jax
import jax.numpy as jnp
from jax import lax

TILE = 128
OCC = 128
NB = 16


def touch_ends(values, rng, least, top_value):
    extent = values.shape
    spot = [jax.random.randint(jax.random.fold_in(rng, axis), (), 0, extent[axis]) for axis in range(len(extent))]
    values = values.at[tuple(spot)].set(least)
    longest = extent.index(max(extent))
    spot[longest] = (spot[longest] + 1) % extent[longest]
    return values.at[tuple(spot)].set(top_value)


def steps_of(key, extent, split, least, high):
    def one(dim, parts):
        heights = jax.random.uniform(jax.random.fold_in(jax.random.fold_in(key, 6), dim), (parts,), jnp.float32, least / len(split), high / len(split))
        return jnp.repeat(jnp.exp(heights), extent[dim] // parts).reshape((-1,) + (1,) * (len(extent) - dim - 1))

    loudness = one(*split[0])
    for cut in split[1:]:
        loudness = loudness * one(*cut)
    return loudness


def scatter_about(own_key, extent, scale, most, cuts=(), kind=jnp.bfloat16):
    loudness = steps_of(own_key, extent, cuts, -0.22, 0.18) if cuts else 1.0
    entries = jax.random.normal(own_key, extent, jnp.float32) * scale * loudness
    return jnp.minimum(jnp.maximum(entries, -most), most).astype(kind)


def setup_inputs(seed: int = 0) -> dict:
    keys = jax.random.split(jax.random.key(seed), 9)
    amplitudes = scatter_about(keys[0], (OCC, OCC, NB * TILE), 1.0, 6.0, ((0, 32), (2, 16)), jnp.float32)
    ladder_ints = scatter_about(keys[1], (NB * TILE, NB * TILE), (NB * TILE // 8) ** -0.5, 0.375, ((0, 16), (1, 32)), jnp.float32)
    cycle_ints = scatter_about(keys[2], (NB * TILE, NB * TILE), (NB * TILE // 8) ** -0.5, 0.375, ((0, 16), (1, 32)), jnp.float32)
    occ_coupling = scatter_about(keys[3], (OCC, OCC), (OCC // 8) ** -0.5, 1.5, (), jnp.float32)
    occ_irrep = touch_ends(jax.random.randint(keys[4], (OCC,), 0, 8), jax.random.fold_in(keys[4], 1), 0, 7).astype(jnp.int32)
    pair_irrep = touch_ends(jax.random.randint(keys[5], (NB,), 0, 8), jax.random.fold_in(keys[5], 1), 0, 7).astype(jnp.int32)
    screen = touch_ends((jax.random.randint(keys[6], (NB, NB), 0, 4) < 3).astype(jnp.int32), jax.random.fold_in(keys[6], 1), 0, 1)
    block_order = jax.random.permutation(keys[7], NB).astype(jnp.int32)
    return dict(amplitudes=amplitudes, ladder_ints=ladder_ints, cycle_ints=cycle_ints, occ_coupling=occ_coupling, occ_irrep=occ_irrep, pair_irrep=pair_irrep, screen=screen, block_order=block_order)


def expand(mask, width):
    return jnp.repeat(jnp.repeat(mask, width, axis=0), width, axis=1)


def reference(amplitudes, ladder_ints, cycle_ints, occ_coupling, occ_irrep, pair_irrep, screen, block_order):
    highest = lax.Precision.HIGHEST
    pair_sym = jnp.bitwise_xor(occ_irrep[:, None], occ_irrep[None, :])
    amp_mask = (pair_sym[:, :, None] == pair_irrep[None, None, :]).astype(jnp.float32)
    amps = amplitudes.reshape(OCC, OCC, NB, TILE) * amp_mask[:, :, :, None]
    amps = amps.reshape(OCC * OCC, NB * TILE)
    same = (pair_irrep[:, None] == pair_irrep[None, :]).astype(jnp.float32)
    ladder_eff = ladder_ints * expand(same * screen.astype(jnp.float32), TILE)
    cycle_eff = cycle_ints * expand(same, TILE)
    coupling = occ_coupling * (occ_irrep[:, None] == occ_irrep[None, :]).astype(jnp.float32)
    ladder = jnp.dot(amps, ladder_eff, precision=highest, preferred_element_type=jnp.float32)
    inner = jnp.dot(amps, cycle_eff, precision=highest, preferred_element_type=jnp.float32)
    cycle = jnp.einsum("ikx,kj->ijx", inner.reshape(OCC, OCC, NB * TILE), coupling, precision=highest)
    resid = ladder.reshape(OCC, OCC, NB * TILE) + cycle
    anti = resid - jnp.transpose(resid, (1, 0, 2))
    ordered = jnp.take(anti.reshape(OCC, OCC, NB, TILE), block_order, axis=2)
    return ordered.reshape(OCC, OCC, NB * TILE)
```

```python
import functools

import jax
import jax.numpy as jnp
from jax import lax
from jax.experimental import pallas as pl
from jax.experimental.pallas import tpu as pltpu
from jax.sharding import PartitionSpec as P

CAP = 32
ROWS = 4
TILE = 128
HIGH = lax.Precision.HIGHEST
NT = (((1,), (1,)), ((), ()))


def split(x):
    hi = x.astype(jnp.bfloat16)
    return hi, (x - hi.astype(jnp.float32)).astype(jnp.bfloat16)


def kernel(
    nz, ny,
    round_s, irr_s, pair_s, screen_s, order_s, irr_v, coup, amps, lad, cyc,
    out, count_s,
    psub, pan, lhs, lhs_hi, lhs_lo, part, xs, xb, ys, yb, res4, full, own, send, back,
    sem_a, sem_b, sem_c, sem_x, sem_y, sem_f, sem_h,
):
    nblk = 4 * nz
    occ = amps.shape[1]
    slots = ROWS * CAP
    g = lax.axis_index("grp")
    b = lax.axis_index("blk")
    z = lax.div(b, 4)
    plane = lax.rem(b, 4)
    h = lax.div(plane, 2)
    c = lax.rem(plane, 2)
    y = lax.div(g, 2)
    xl = lax.rem(g, 2)
    x_dev = z * 4 + (1 - h) * 2 + c
    c_dev = z * 4 + h * 2 + (1 - c)
    x_plane = (1 - h) * 2 + c

    barrier = pltpu.get_barrier_semaphore()

    def greet_blk(d, carry):
        pl.semaphore_signal(
            barrier, inc=1, device_id={"blk": lax.rem(b + d, nblk)}, device_id_type=pl.DeviceIdType.MESH
        )
        return carry

    lax.fori_loop(1, nblk, greet_blk, 0)

    def greet_grp(d, carry):
        pl.semaphore_signal(
            barrier, inc=1, device_id={"grp": lax.rem(y + d, ny) * 2 + xl}, device_id_type=pl.DeviceIdType.MESH
        )
        return carry

    lax.fori_loop(1, ny, greet_grp, 0)
    pl.semaphore_signal(
        barrier, inc=1, device_id={"grp": y * 2 + 1 - xl}, device_id_type=pl.DeviceIdType.MESH
    )

    my_label = pair_s[g]
    tile_id = lax.div(b, 2)
    same = jnp.where(pair_s[tile_id] == my_label, 1.0, 0.0)
    kept = same * screen_s[g, tile_id].astype(jnp.float32)
    lad_t = lad[...].T * kept
    cyc_t = cyc[...].T * same
    for s in range(2):
        psub[s, :, 0:TILE] = lad_t[32 * s : 32 * s + 32]
        psub[s, :, TILE : 2 * TILE] = cyc_t[32 * s : 32 * s + 32]
    pan[z, h] = psub[h]

    irr_b = jnp.broadcast_to(irr_v[...].astype(jnp.float32), (occ, occ))
    irr_t = irr_b.T
    equal = irr_b == irr_t
    before = lax.broadcasted_iota(jnp.int32, (occ, occ), 0) < lax.broadcasted_iota(
        jnp.int32, (occ, occ), 1
    )
    rank = jnp.sum(jnp.where(equal & before, 1.0, 0.0), axis=0, keepdims=True)
    key = irr_v[...].astype(jnp.float32) * occ + rank
    count_s[0] = jnp.max(rank).astype(jnp.int32) + 1

    def targets(label, place):
        goal = place.astype(jnp.float32)
        for i in reversed(range(ROWS)):
            base = (irr_s[b * ROWS + i] ^ label) * occ + round_s[0] * CAP - CAP * i
            at = place.astype(jnp.float32) + base.astype(jnp.float32)
            goal = at if i == ROWS - 1 else jnp.where(place < CAP * (i + 1), at, goal)
        return goal

    key_b = jnp.broadcast_to(key, (slots, occ))
    sel = jnp.where(
        key_b == targets(my_label, lax.broadcasted_iota(jnp.int32, (slots, occ), 0)), 1.0, 0.0
    )
    coupling = jnp.where(equal, coup[...], 0.0)
    sel_c = lax.dot_general(sel, coupling, NT, precision=HIGH, preferred_element_type=jnp.float32)
    for i in range(ROWS):
        rows = slice(CAP * i, CAP * i + CAP)
        pick = jnp.concatenate((sel[rows], sel_c[rows]), axis=0)
        packed = jnp.dot(pick, amps[i], precision=HIGH, preferred_element_type=jnp.float32)
        lhs[plane, rows, 0:TILE] = packed[:CAP]
        lhs[plane, rows, TILE : 2 * TILE] = packed[CAP:]

    pl.semaphore_wait(barrier, nblk - 1 + ny)

    def remote(src, dst, sems, index, where):
        return pltpu.make_async_remote_copy(
            src_ref=src,
            dst_ref=dst,
            send_sem=sems.at[(0, *index)],
            recv_sem=sems.at[(1, *index)],
            device_id=where,
            device_id_type=pl.DeviceIdType.MESH,
        )

    def to_x():
        return remote(psub.at[1 - h], pan.at[z, h], sem_b, (0,), {"blk": x_dev})

    def from_x():
        return remote(psub.at[1 - h], pan.at[z, 1 - h], sem_b, (0,), {"blk": x_dev})

    def along_z(which, k, d):
        return remote(
            pan.at[z, which], pan.at[z, which], sem_c, (k, d), {"blk": lax.rem(z + d, nz) * 4 + plane}
        )

    def rows_to(src, where, k):
        return remote(lhs.at[src], lhs.at[src], sem_a, (k,), {"blk": where})

    to_x().start()
    rows_to(plane, x_dev, 0).start()

    def start_own(d, carry):
        along_z(h, 0, d).start()
        return carry

    lax.fori_loop(1, nz, start_own, 0)
    rows_to(plane, c_dev, 1).start()
    from_x().wait_recv()

    def start_other(d, carry):
        along_z(1 - h, 1, d).start()
        return carry

    lax.fori_loop(1, nz, start_other, 0)
    rows_to(x_plane, x_dev, 0).wait_recv()
    rows_to(x_plane, c_dev, 2).start()
    rows_to(h * 2 + 1 - c, c_dev, 1).wait_recv()
    rows_to((1 - h) * 2 + 1 - c, c_dev, 2).wait_recv()
    hi, lo = split(lhs[...].reshape(4 * slots, 2 * TILE))
    lhs_hi[...] = hi
    lhs_lo[...] = lo

    def multiply(src):
        hi, lo = split(pan[src].reshape(64, 2 * TILE))
        value = lax.dot_general(hi, lhs_hi[...], NT, preferred_element_type=jnp.float32)
        value += lax.dot_general(hi, lhs_lo[...], NT, preferred_element_type=jnp.float32)
        value += lax.dot_general(lo, lhs_hi[...], NT, preferred_element_type=jnp.float32)
        part[src * 2] = value[:32]
        part[src * 2 + 1] = value[32:]

    multiply(z)

    def take_z(d, carry):
        src = lax.rem(z + nz - d, nz)
        remote(pan.at[z, h], pan.at[src, h], sem_c, (0, d), {"blk": x_dev}).wait_recv()
        remote(pan.at[z, h], pan.at[src, 1 - h], sem_c, (1, d), {"blk": x_dev}).wait_recv()
        multiply(src)
        return carry

    lax.fori_loop(1, nz, take_z, 0)

    def pair_copy(k):
        return remote(xs.at[k], xb.at[k], sem_x, (k,), {"grp": y * 2 + 1 - xl})

    def y_copy(k):
        return remote(ys.at[k], yb.at[k], sem_y, (k,), {"grp": lax.rem(y + k, ny) * 2 + xl})

    def send_x(n, carry):
        k = lax.rem(n + 1, ny)
        xs[k] = part[order_s[lax.rem(y + k, ny) * 2 + 1 - xl]]
        pair_copy(k).start()
        return carry

    lax.fori_loop(0, ny, send_x, 0)

    def send_y(k, carry):
        pair_copy(k).wait_recv()
        ys[k] = part[order_s[lax.rem(y + k, ny) * 2 + xl]] + xb[k]
        y_copy(k).start()
        return carry

    lax.fori_loop(1, ny, send_y, 0)
    pair_copy(0).wait_recv()
    total = part[order_s[g]] + xb[0]

    def take_y(k, total):
        y_copy(k).wait_recv()
        return total + yb[k]

    total = lax.fori_loop(1, ny, take_y, total)

    quarter = c * 2 + h
    for r in range(4):
        res4[r] = total[:, slots * r : slots * (r + 1)]

    def plane_copy(d):
        to = lax.rem(plane + d, 4)
        return remote(res4.at[to], full.at[quarter], sem_f, (d,), {"blk": z * 4 + to})

    for d in range(1, 4):
        plane_copy(d).start()
    full[quarter] = res4[plane]

    out_label = pair_s[order_s[g]]
    key_t = jnp.broadcast_to(key, (slots, occ)).T
    lane = lax.broadcasted_iota(jnp.int32, (occ, slots), 1)
    place = jnp.where(key_t == targets(out_label, lane), 1.0, 0.0)
    for d in range(1, 4):
        other = lax.rem(plane + 4 - d, 4)
        other_quarter = lax.rem(other, 2) * 2 + lax.div(other, 2)
        remote(res4.at[0], full.at[other_quarter], sem_f, (d,), {"blk": c_dev}).wait_recv()
    full_t = full[...].reshape(TILE, slots).T
    for i in range(ROWS):
        mine = (lane >= CAP * i) & (lane < CAP * (i + 1))
        value = jnp.dot(
            jnp.where(mine, place, 0.0), full_t, precision=HIGH, preferred_element_type=jnp.float32
        )
        own[i] = value
        send[pl.ds(i, occ, stride=ROWS), :] = value

    def swap(d):
        to = lax.rem(b + d, nblk)
        return remote(
            send.at[pl.ds(pl.multiple_of(to * 16, 16), 16)],
            back.at[pl.ds(pl.multiple_of(b * 16, 16), 16)],
            sem_h,
            (d,),
            {"blk": to},
        )

    def start_swap(d, carry):
        swap(d).start()
        return carry

    lax.fori_loop(1, nblk, start_swap, 0)
    here = pl.ds(pl.multiple_of(b * 16, 16), 16)
    back[here] = send[here]

    def take_swap(d, carry):
        src = lax.rem(b + nblk - d, nblk)
        remote(
            send.at[here], back.at[pl.ds(pl.multiple_of(src * 16, 16), 16)], sem_h, (d,), {"blk": c_dev}
        ).wait_recv()
        return carry

    lax.fori_loop(1, nblk, take_swap, 0)
    for j in range(ROWS):
        for i in range(ROWS):
            at = pl.ds(i, nblk, stride=ROWS)
            out[j, at, :] = own[j, at, :] - back[pl.ds(ROWS * j + i, nblk, stride=16), :]

    to_x().wait_send()
    rows_to(plane, x_dev, 0).wait_send()
    rows_to(plane, c_dev, 1).wait_send()
    rows_to(x_plane, c_dev, 2).wait_send()

    def end_z(d, carry):
        along_z(h, 0, d).wait_send()
        along_z(1 - h, 1, d).wait_send()
        return carry

    lax.fori_loop(1, nz, end_z, 0)
    pair_copy(0).wait_send()

    def end_y(k, carry):
        pair_copy(k).wait_send()
        y_copy(k).wait_send()
        return carry

    lax.fori_loop(1, ny, end_y, 0)
    for d in range(1, 4):
        plane_copy(d).wait_send()

    def end_swap(d, carry):
        swap(d).wait_send()
        return carry

    lax.fori_loop(1, nblk, end_swap, 0)


def shards(
    amplitudes, ladder_ints, cycle_ints, occ_coupling, occ_irrep, pair_irrep, screen, block_order
):
    rows, occ, tile = amplitudes.shape
    nz = lax.axis_size("blk") // 4
    ny = lax.axis_size("grp") // 2
    slots = ROWS * CAP
    f32 = jnp.float32
    smem = pl.BlockSpec(memory_space=pltpu.SMEM)
    vmem = pl.BlockSpec(memory_space=pltpu.VMEM)
    dma = pltpu.SemaphoreType.DMA
    call = pl.pallas_call(
        functools.partial(kernel, nz, ny),
        out_shape=(
            jax.ShapeDtypeStruct((rows, occ, tile), f32),
            jax.ShapeDtypeStruct((1,), jnp.int32),
        ),
        in_specs=[smem] * 5 + [vmem] * 5,
        out_specs=(vmem, smem),
        scratch_shapes=[
            pltpu.VMEM((2, 32, 2 * TILE), f32),
            pltpu.VMEM((nz, 2, 32, 2 * TILE), f32),
            pltpu.VMEM((4, slots, 2 * TILE), f32),
            pltpu.VMEM((4 * slots, 2 * TILE), jnp.bfloat16),
            pltpu.VMEM((4 * slots, 2 * TILE), jnp.bfloat16),
            pltpu.VMEM((2 * nz, 32, 4 * slots), f32),
            pltpu.VMEM((ny, 32, 4 * slots), f32),
            pltpu.VMEM((ny, 32, 4 * slots), f32),
            pltpu.VMEM((ny, 32, 4 * slots), f32),
            pltpu.VMEM((ny, 32, 4 * slots), f32),
            pltpu.VMEM((4, 32, slots), f32),
            pltpu.VMEM((4, 32, slots), f32),
            pltpu.VMEM((rows, occ, tile), f32),
            pltpu.VMEM((rows * occ, tile), f32),
            pltpu.VMEM((rows * occ, tile), f32),
            dma((2, 3)),
            dma((2, 1)),
            dma((2, 2, nz)),
            dma((2, ny)),
            dma((2, ny)),
            dma((2, 4)),
            dma((2, 4 * nz)),
        ],
        compiler_params=pltpu.CompilerParams(
            collective_id=0, has_side_effects=True, vmem_limit_bytes=24 << 20
        ),
    )

    def part(index):
        return call(
            jnp.full((1,), index, jnp.int32),
            occ_irrep, pair_irrep, screen, block_order, occ_irrep.reshape(1, occ),
            occ_coupling, amplitudes, ladder_ints, cycle_ints,
        )

    first, count = part(0)
    rounds = (count[0] + CAP - 1) // CAP

    def more(state):
        return state[0] < rounds

    def again(state):
        return state[0] + 1, state[1] + part(state[0])[0]

    return lax.while_loop(more, again, (jnp.int32(1), first))[1]


def solution(mesh):
    placed = (P("blk", None, "grp"), P("grp", "blk"), P("grp", "blk"), P(), P(), P(), P(), P())
    return jax.shard_map(
        shards, mesh=mesh, in_specs=placed, out_specs=P("blk", None, "grp"), check_vma=False
    )
```

```python
import functools

import jax
import jax.numpy as jnp
from jax import lax
from jax.experimental import pallas as pl
from jax.experimental.pallas import tpu as pltpu
from jax.sharding import PartitionSpec as P

CAP = 32
JOINT = 384
ROWS = 4
TILE = 128
HIGH = lax.Precision.HIGHEST
NT = (((1,), (1,)), ((), ()))


def split(x):
    hi = x.astype(jnp.bfloat16)
    return hi, (x - hi.astype(jnp.float32)).astype(jnp.bfloat16)


def kernel(
    nz, ny,
    *refs,
):
    given, (out, count_s), held = refs[:10], refs[10:12], refs[12:22]
    round_s, irr_s, pair_s, screen_s, order_s, irr_v, coup, amps, lad, cyc = held
    (
        psub, pan, lhs, lhs_hi, lhs_lo, pack, part, xs, xb, ys, yb, res4, full, own, send, back,
        sem_in, sem_a, sem_b, sem_c, sem_x, sem_y, sem_f, sem_h,
    ) = refs[22:]
    nblk = 4 * nz
    occ = amps.shape[1]
    slots = ROWS * CAP
    g = lax.axis_index("grp")
    b = lax.axis_index("blk")
    z = lax.div(b, 4)
    plane = lax.rem(b, 4)
    h = lax.div(plane, 2)
    c = lax.rem(plane, 2)
    y = lax.div(g, 2)
    xl = lax.rem(g, 2)
    x_dev = z * 4 + (1 - h) * 2 + c
    c_dev = z * 4 + h * 2 + (1 - c)
    x_plane = (1 - h) * 2 + c

    barrier = pltpu.get_barrier_semaphore()

    def greet(where):
        pl.semaphore_signal(barrier, inc=1, device_id=where, device_id_type=pl.DeviceIdType.MESH)

    def z_dev(d):
        return {"blk": lax.rem(z + nz + d, nz) * 4 + plane}

    def y_dev(d):
        return {"grp": lax.rem(y + ny + d, ny) * 2 + xl}

    x_pair = {"grp": y * 2 + 1 - xl}
    for d in range(1, 4):
        greet({"blk": z * 4 + lax.rem(plane + d, 4)})
    for d in (1, -1):
        greet(z_dev(d))
        greet({"blk": lax.rem(z + nz + d, nz) * 4 + x_plane})
    greet(x_pair)
    for d in range(1, ny):
        greet(y_dev(d))

    def fetch(n):
        return pltpu.make_async_copy(given[n], held[n], sem_in.at[n])

    for n in range(10):
        fetch(n).start()
    for n in range(10):
        fetch(n).wait()

    my_label = pair_s[g]
    tile_id = lax.div(b, 2)
    same = jnp.where(pair_s[tile_id] == my_label, 1.0, 0.0)
    kept = same * screen_s[g, tile_id].astype(jnp.float32)
    lad_t = lad[...] * kept
    cyc_t = cyc[...] * same
    for s in range(2):
        psub[s, :, 0:TILE] = lad_t[32 * s : 32 * s + 32]
        psub[s, :, TILE : 2 * TILE] = cyc_t[32 * s : 32 * s + 32]
    pan[z, h] = psub[h]

    irr_b = jnp.broadcast_to(irr_v[...].astype(jnp.float32), (occ, occ))
    irr_t = irr_b.T
    equal = irr_b == irr_t
    before = lax.broadcasted_iota(jnp.int32, (occ, occ), 0) < lax.broadcasted_iota(
        jnp.int32, (occ, occ), 1
    )
    rank = jnp.sum(jnp.where(equal & before, 1.0, 0.0), axis=0, keepdims=True)
    key = irr_v[...].astype(jnp.float32) * occ + rank
    irr_bi = irr_b.astype(jnp.int32)
    irr_ti = irr_t.astype(jnp.int32)
    plane_of = lax.broadcasted_iota(jnp.int32, (8, occ), 0) == lax.div(
        lax.broadcasted_iota(jnp.int32, (8, occ), 1), 4 * ROWS
    )
    plane_of = jnp.where(plane_of, 1.0, 0.0)
    worst = jnp.zeros((8, occ), jnp.float32)
    for label in range(8):
        hit = ((irr_bi ^ irr_ti) == label) & (rank < CAP)
        filled = jnp.dot(
            plane_of.astype(jnp.bfloat16),
            jnp.where(hit, 1.0, 0.0).astype(jnp.bfloat16),
            preferred_element_type=jnp.float32,
        )
        worst = jnp.maximum(worst, jnp.sum(filled, axis=1, keepdims=True))
    count_s[0] = lax.div(jnp.max(rank).astype(jnp.int32) + CAP, CAP)
    count_s[1] = lax.div(jnp.max(worst).astype(jnp.int32) + JOINT - 1, JOINT)
    first_rank = (round_s[0] * CAP).astype(jnp.float32)

    def joint_of(label):
        lane = lax.broadcasted_iota(jnp.int32, (1, 4 * slots), 1)
        row_of, slot_of = lax.div(lane, CAP), lax.rem(lane, CAP).astype(jnp.float32)
        irr_f = irr_v[...].astype(jnp.float32)
        goal = jnp.full((1, 4 * slots), -1.0, jnp.float32)
        start = jnp.full((1, 1), 0.0, jnp.float32) - (round_s[1] * JOINT).astype(jnp.float32)
        for row in range(4 * ROWS):
            want = (irr_s[z * 4 * ROWS + row] ^ label).astype(jnp.float32)
            fits = (irr_f == want) & (rank >= first_rank) & (rank < first_rank + CAP)
            size = jnp.sum(jnp.where(fits, 1.0, 0.0), axis=1, keepdims=True)
            goal = jnp.where((row_of == row) & (slot_of < size), start + slot_of, goal)
            start = start + size
        at = lax.broadcasted_iota(jnp.int32, (JOINT, 4 * slots), 0).astype(jnp.float32)
        return jnp.where(at == jnp.broadcast_to(goal, at.shape), 1.0, 0.0).astype(jnp.bfloat16)

    def targets(label, place):
        goal = place.astype(jnp.float32)
        for i in reversed(range(ROWS)):
            base = (irr_s[b * ROWS + i] ^ label) * occ + round_s[0] * CAP - CAP * i
            at = place.astype(jnp.float32) + base.astype(jnp.float32)
            goal = at if i == ROWS - 1 else jnp.where(place < CAP * (i + 1), at, goal)
        return goal

    key_b = jnp.broadcast_to(key, (slots, occ))
    sel = jnp.where(
        key_b == targets(my_label, lax.broadcasted_iota(jnp.int32, (slots, occ), 0)), 1.0, 0.0
    )
    coupling = jnp.where(equal, coup[...], 0.0)
    sel_c = lax.dot_general(sel, coupling, NT, precision=HIGH, preferred_element_type=jnp.float32)
    for i in range(ROWS):
        rows = slice(CAP * i, CAP * i + CAP)
        pick = jnp.concatenate((sel[rows], sel_c[rows]), axis=0)
        packed = jnp.dot(pick, amps[i], precision=HIGH, preferred_element_type=jnp.float32)
        lhs[plane, rows, 0:TILE] = packed[:CAP]
        lhs[plane, rows, TILE : 2 * TILE] = packed[CAP:]

    pack[...] = joint_of(my_label)
    pl.semaphore_wait(barrier, 8 + ny - 1)

    def remote(src, dst, sems, index, where):
        return pltpu.make_async_remote_copy(
            src_ref=src,
            dst_ref=dst,
            send_sem=sems.at[(0, *index)],
            recv_sem=sems.at[(1, *index)],
            device_id=where,
            device_id_type=pl.DeviceIdType.MESH,
        )

    def to_x():
        return remote(psub.at[1 - h], pan.at[z, h], sem_b, (0,), {"blk": x_dev})

    def from_x():
        return remote(psub.at[1 - h], pan.at[z, 1 - h], sem_b, (0,), {"blk": x_dev})

    def to_x_z(way):
        step = 1 - 2 * way
        return remote(
            psub.at[1 - h], pan.at[z, h], sem_c, (1, way, 1),
            {"blk": lax.rem(z + nz + step, nz) * 4 + x_plane},
        )

    tiles = (h, 1 - h)
    reach = ((nz // 2, nz - 1 - nz // 2), (nz - 1 - nz // 2, nz // 2))

    def pass_z(kind, way, t):
        step = 1 - 2 * way
        src = lax.rem(z + nz - step * (t - 1), nz)
        at = pan.at[src, tiles[kind]]
        return remote(at, at, sem_c, (kind, way, t), z_dev(step))

    def got_z(kind, way, t):
        step = 1 - 2 * way
        src = lax.rem(z + nz - step * t, nz)
        at = pan.at[src, tiles[kind]]
        return remote(at, at, sem_c, (kind, way, t), z_dev(step))

    def start_z(kind, t):
        for way in range(2):
            if t <= reach[kind][way]:
                if t > 1:
                    got_z(kind, way, t - 1).wait_recv()
                pass_z(kind, way, t).start()

    def rows_to(src, where, k):
        return remote(lhs.at[src], lhs.at[src], sem_a, (k,), {"blk": where})

    to_x().start()
    for way in range(2):
        if reach[1][way]:
            to_x_z(way).start()
    start_z(0, 1)
    rows_to(plane, x_dev, 0).start()
    rows_to(plane, c_dev, 1).start()
    for t in range(2, 4):
        for kind in range(2):
            start_z(kind, t)
    from_x().wait_recv()
    rows_to(x_plane, x_dev, 0).wait_recv()
    rows_to(x_plane, c_dev, 2).start()
    rows_to(h * 2 + 1 - c, c_dev, 1).wait_recv()
    rows_to((1 - h) * 2 + 1 - c, c_dev, 2).wait_recv()
    hi, lo = split(lhs[...].reshape(4 * slots, 2 * TILE))
    lhs_hi[...] = jnp.dot(pack[...], hi, preferred_element_type=jnp.float32).astype(jnp.bfloat16)
    lhs_lo[...] = jnp.dot(pack[...], lo, preferred_element_type=jnp.float32).astype(jnp.bfloat16)
    out_label = pair_s[order_s[g]]
    pack[...] = joint_of(out_label)

    def multiply(src):
        hi, lo = split(pan[src].reshape(64, 2 * TILE))
        value = lax.dot_general(hi, lhs_hi[...], NT, preferred_element_type=jnp.float32)
        value += lax.dot_general(hi, lhs_lo[...], NT, preferred_element_type=jnp.float32)
        value += lax.dot_general(lo, lhs_hi[...], NT, preferred_element_type=jnp.float32)
        part[src * 2] = value[:32]
        part[src * 2 + 1] = value[32:]

    multiply(z)
    for t in range(1, nz // 2 + 1):
        for kind in range(2):
            if t == 1 and nz // 2 >= 4:
                for more in range(4, nz // 2 + 1):
                    start_z(kind, more)
        for way in range(2):
            for kind in range(2):
                if t == reach[kind][way]:
                    got_z(kind, way, t).wait_recv()
        multiply(lax.rem(z + nz - t, nz))
        if 2 * t < nz:
            multiply(lax.rem(z + t, nz))

    def pair_copy(k):
        return remote(xs.at[k], xb.at[k], sem_x, (k,), x_pair)

    def y_copy(k):
        return remote(ys.at[k], yb.at[k], sem_y, (k,), y_dev(k))

    def owner(k):
        return lax.rem(y + k, ny) * 2

    order = []
    for far in range(ny // 2, 0, -1):
        order += [far] if 2 * far == ny else [far, ny - far]
    for k in order + [0]:
        xs[k] = part[order_s[owner(k) + 1 - xl]]
        pair_copy(k).start()
    for k in order:
        pair_copy(k).wait_recv()
        ys[k] = part[order_s[owner(k) + xl]] + xb[k]
        y_copy(k).start()
    pair_copy(0).wait_recv()
    total = part[order_s[g]] + xb[0]
    for k in order:
        y_copy(k).wait_recv()
        total += yb[k]
    hi, lo = split(total)
    total = jnp.dot(hi, pack[...], preferred_element_type=jnp.float32)
    total += jnp.dot(lo, pack[...], preferred_element_type=jnp.float32)

    quarter = c * 2 + h
    for r in range(4):
        res4[r] = total[:, slots * r : slots * (r + 1)]

    def plane_copy(d):
        to = lax.rem(plane + d, 4)
        return remote(res4.at[to], full.at[quarter], sem_f, (d,), {"blk": z * 4 + to})

    for d in range(1, 4):
        plane_copy(d).start()
    full[quarter] = res4[plane]

    key_t = jnp.broadcast_to(key, (slots, occ)).T
    lane = lax.broadcasted_iota(jnp.int32, (occ, slots), 1)
    place = jnp.where(key_t == targets(out_label, lane), 1.0, 0.0)
    for d in range(1, 4):
        other = lax.rem(plane + 4 - d, 4)
        other_quarter = lax.rem(other, 2) * 2 + lax.div(other, 2)
        remote(res4.at[0], full.at[other_quarter], sem_f, (d,), {"blk": c_dev}).wait_recv()
    full_t = full[...].reshape(TILE, slots).T
    for i in range(ROWS):
        mine = (lane >= CAP * i) & (lane < CAP * (i + 1))
        value = jnp.dot(
            jnp.where(mine, place, 0.0), full_t, precision=HIGH, preferred_element_type=jnp.float32
        )
        own[i] = value
        send[pl.ds(i, occ, stride=ROWS), :] = value

    def swap(d):
        to = lax.rem(b + d, nblk)
        return remote(
            send.at[pl.ds(pl.multiple_of(to * 16, 16), 16)],
            back.at[pl.ds(pl.multiple_of(b * 16, 16), 16)],
            sem_h,
            (d,),
            {"blk": to},
        )

    def start_swap(n, carry):
        odd = lax.rem(n, 2)
        half = lax.div(n, 2)
        swap(odd * (half + 1) + (1 - odd) * (nblk - half)).start()
        return carry

    lax.fori_loop(1, nblk, start_swap, 0)
    here = pl.ds(pl.multiple_of(b * 16, 16), 16)
    back[here] = send[here]

    def take_swap(d, carry):
        src = lax.rem(b + nblk - d, nblk)
        remote(
            send.at[here], back.at[pl.ds(pl.multiple_of(src * 16, 16), 16)], sem_h, (d,), {"blk": c_dev}
        ).wait_recv()
        return carry

    lax.fori_loop(1, nblk, take_swap, 0)
    for j in range(ROWS):
        for i in range(ROWS):
            at = pl.ds(i, nblk, stride=ROWS)
            out[j, at, :] = own[j, at, :] - back[pl.ds(ROWS * j + i, nblk, stride=16), :]

    to_x().wait_send()
    rows_to(plane, x_dev, 0).wait_send()
    rows_to(plane, c_dev, 1).wait_send()
    rows_to(x_plane, c_dev, 2).wait_send()

    for kind in range(2):
        for way in range(2):
            for t in range(1, reach[kind][way] + 1):
                (to_x_z(way) if (kind, t) == (1, 1) else pass_z(kind, way, t)).wait_send()
    for k in order + [0]:
        pair_copy(k).wait_send()
    for k in order:
        y_copy(k).wait_send()
    for d in range(1, 4):
        plane_copy(d).wait_send()

    def end_swap(d, carry):
        swap(d).wait_send()
        return carry

    lax.fori_loop(1, nblk, end_swap, 0)


def shards(
    amplitudes, ladder_ints, cycle_ints, occ_coupling, occ_irrep, pair_irrep, screen, block_order
):
    rows, occ, tile = amplitudes.shape
    nz = lax.axis_size("blk") // 4
    ny = lax.axis_size("grp") // 2
    slots = ROWS * CAP
    f32 = jnp.float32
    smem = pl.BlockSpec(memory_space=pltpu.SMEM)
    vmem = pl.BlockSpec(memory_space=pltpu.VMEM)
    dma = pltpu.SemaphoreType.DMA
    call = pl.pallas_call(
        functools.partial(kernel, nz, ny),
        out_shape=(
            jax.ShapeDtypeStruct((rows, occ, tile), f32),
            jax.ShapeDtypeStruct((2,), jnp.int32),
        ),
        in_specs=[pl.BlockSpec(memory_space=pltpu.HBM)] * 10,
        out_specs=(vmem, smem),
        scratch_shapes=[
            pltpu.SMEM((2,), jnp.int32),
            pltpu.SMEM(occ_irrep.shape, jnp.int32),
            pltpu.SMEM(pair_irrep.shape, jnp.int32),
            pltpu.SMEM(screen.shape, jnp.int32),
            pltpu.SMEM(block_order.shape, jnp.int32),
            pltpu.VMEM((1, occ), jnp.int32),
            pltpu.VMEM((occ, occ), f32),
            pltpu.VMEM((rows, occ, tile), f32),
            pltpu.VMEM(ladder_ints.shape[::-1], f32),
            pltpu.VMEM(cycle_ints.shape[::-1], f32),
            pltpu.VMEM((2, 32, 2 * TILE), f32),
            pltpu.VMEM((nz, 2, 32, 2 * TILE), f32),
            pltpu.VMEM((4, slots, 2 * TILE), f32),
            pltpu.VMEM((JOINT, 2 * TILE), jnp.bfloat16),
            pltpu.VMEM((JOINT, 2 * TILE), jnp.bfloat16),
            pltpu.VMEM((JOINT, 4 * slots), jnp.bfloat16),
            pltpu.VMEM((2 * nz, 32, JOINT), f32),
            pltpu.VMEM((ny, 32, JOINT), f32),
            pltpu.VMEM((ny, 32, JOINT), f32),
            pltpu.VMEM((ny, 32, JOINT), f32),
            pltpu.VMEM((ny, 32, JOINT), f32),
            pltpu.VMEM((4, 32, slots), f32),
            pltpu.VMEM((4, 32, slots), f32),
            pltpu.VMEM((rows, occ, tile), f32),
            pltpu.VMEM((rows * occ, tile), f32),
            pltpu.VMEM((rows * occ, tile), f32),
            dma((10,)),
            dma((2, 3)),
            dma((2, 1)),
            dma((2, 2, 2, nz // 2 + 1)),
            dma((2, ny)),
            dma((2, ny)),
            dma((2, 4)),
            dma((2, 4 * nz)),
        ],
        compiler_params=pltpu.CompilerParams(
            collective_id=0, has_side_effects=True, vmem_limit_bytes=24 << 20
        ),
    )

    def part(index):
        return call(
            index,
            occ_irrep, pair_irrep, screen, block_order, occ_irrep.reshape(1, occ),
            occ_coupling, amplitudes, ladder_ints.T, cycle_ints.T,
        )

    first, count = part(jnp.zeros((2,), jnp.int32))
    passes = count[0] * count[1]

    def more(state):
        return state[0] < passes

    def again(state):
        index = jnp.stack((state[0] // count[1], state[0] % count[1]))
        return state[0] + 1, state[1] + part(index)[0]

    return lax.while_loop(more, again, (jnp.int32(1), first))[1]


def solution(mesh):
    placed = (P("blk", None, "grp"), P("grp", "blk"), P("grp", "blk"), P(), P(), P(), P(), P())
    return jax.shard_map(
        shards, mesh=mesh, in_specs=placed, out_specs=P("blk", None, "grp"), check_vma=False
    )
```

```python
import functools

import jax
import jax.numpy as jnp
import numpy as np
from jax import lax
from jax.experimental import pallas as pl
from jax.experimental.pallas import tpu as pltpu
from jax.sharding import PartitionSpec as P

CAP = 32
JOINT = 384
ROWS = 4
TILE = 128
NT = (((1,), (1,)), ((), ()))
NN = (((1,), (0,)), ((), ()))


def split(x):
    hi = x.astype(jnp.bfloat16)
    return hi, (x - hi.astype(jnp.float32)).astype(jnp.bfloat16)


def product(a, b, dims):
    a_hi, a_lo = split(a)
    b_hi, b_lo = split(b)
    value = lax.dot_general(a_hi, b_hi, dims, preferred_element_type=jnp.float32)
    value += lax.dot_general(a_hi, b_lo, dims, preferred_element_type=jnp.float32)
    return value + lax.dot_general(a_lo, b_hi, dims, preferred_element_type=jnp.float32)


def kernel(
    nz, ny,
    *refs,
):
    given, (out, count_s), held = refs[:10], refs[10:12], refs[12:22]
    round_s, irr_s, pair_s, screen_s, order_s, irr_v, coup, amps, lad, cyc = held
    (
        psub, pan, lhs, lhs_hi, lhs_lo, pack, place, part, xs, xb, ys, yb, res4, full, own, send, back,
        sem_in, sem_a, sem_b, sem_c, sem_x, sem_y, sem_f, sem_h,
    ) = refs[22:]
    nblk = 4 * nz
    occ = amps.shape[1]
    slots = ROWS * CAP
    g = lax.axis_index("grp")
    b = lax.axis_index("blk")
    z = lax.div(b, 4)
    plane = lax.rem(b, 4)
    h = lax.div(plane, 2)
    c = lax.rem(plane, 2)
    y = lax.div(g, 2)
    xl = lax.rem(g, 2)
    x_dev = z * 4 + (1 - h) * 2 + c
    c_dev = z * 4 + h * 2 + (1 - c)
    x_plane = (1 - h) * 2 + c

    barrier = pltpu.get_barrier_semaphore()

    def greet(where):
        pl.semaphore_signal(barrier, inc=1, device_id=where, device_id_type=pl.DeviceIdType.MESH)

    def z_dev(d):
        return {"blk": lax.rem(z + nz + d, nz) * 4 + plane}

    def y_dev(d):
        return {"grp": lax.rem(y + ny + d, ny) * 2 + xl}

    x_pair = {"grp": y * 2 + 1 - xl}
    for d in range(1, 4):
        greet({"blk": z * 4 + lax.rem(plane + d, 4)})
    for d in (1, -1):
        greet(z_dev(d))
        greet({"blk": lax.rem(z + nz + d, nz) * 4 + x_plane})
    greet(x_pair)
    for d in range(1, ny):
        greet(y_dev(d))

    def fetch(n):
        return pltpu.make_async_copy(given[n], held[n], sem_in.at[n])

    for n in (8, 9, 2, 3, 1, 4, 0, 5, 6, 7):
        fetch(n).start()
    for n in (2, 3, 8, 9):
        fetch(n).wait()

    my_label = pair_s[g]
    tile_id = lax.div(b, 2)
    same = jnp.where(pair_s[tile_id] == my_label, 1.0, 0.0)
    kept = same * screen_s[g, tile_id].astype(jnp.float32)
    lad_t = lad[...] * kept
    cyc_t = cyc[...] * same
    for s in range(2):
        psub[s, :, 0:TILE] = lad_t[32 * s : 32 * s + 32]
        psub[s, :, TILE : 2 * TILE] = cyc_t[32 * s : 32 * s + 32]
    pan[z, h] = psub[h]

    pl.semaphore_wait(barrier, 8 + ny - 1)

    def remote(src, dst, sems, index, where):
        return pltpu.make_async_remote_copy(
            src_ref=src,
            dst_ref=dst,
            send_sem=sems.at[(0, *index)],
            recv_sem=sems.at[(1, *index)],
            device_id=where,
            device_id_type=pl.DeviceIdType.MESH,
        )

    def to_x():
        return remote(psub.at[1 - h], pan.at[z, h], sem_b, (0,), {"blk": x_dev})

    def from_x():
        return remote(psub.at[1 - h], pan.at[z, 1 - h], sem_b, (0,), {"blk": x_dev})

    def to_x_z(way):
        step = 1 - 2 * way
        return remote(
            psub.at[1 - h], pan.at[z, h], sem_c, (1, way, 1),
            {"blk": lax.rem(z + nz + step, nz) * 4 + x_plane},
        )

    tiles = (h, 1 - h)
    reach = ((nz // 2, nz - 1 - nz // 2), (nz - 1 - nz // 2, nz // 2))

    def pass_z(kind, way, t):
        step = 1 - 2 * way
        src = lax.rem(z + nz - step * (t - 1), nz)
        at = pan.at[src, tiles[kind]]
        return remote(at, at, sem_c, (kind, way, t), z_dev(step))

    def got_z(kind, way, t):
        step = 1 - 2 * way
        src = lax.rem(z + nz - step * t, nz)
        at = pan.at[src, tiles[kind]]
        return remote(at, at, sem_c, (kind, way, t), z_dev(step))

    def start_z(kind, t):
        for way in range(2):
            if t <= reach[kind][way]:
                if t > 1:
                    got_z(kind, way, t - 1).wait_recv()
                pass_z(kind, way, t).start()

    def rows_to(src, where, k):
        return remote(lhs.at[src], lhs.at[src], sem_a, (k,), {"blk": where})

    to_x().start()
    for way in range(2):
        if reach[1][way]:
            to_x_z(way).start()
    start_z(0, 1)
    for n in (0, 1, 4, 5, 6, 7):
        fetch(n).wait()

    irr_b = jnp.broadcast_to(irr_v[...].astype(jnp.float32), (occ, occ))
    irr_t = irr_b.T
    equal = irr_b == irr_t
    before = lax.broadcasted_iota(jnp.int32, (occ, occ), 0) < lax.broadcasted_iota(
        jnp.int32, (occ, occ), 1
    )
    rank = jnp.sum(jnp.where(equal & before, 1.0, 0.0), axis=0, keepdims=True)
    key = irr_v[...].astype(jnp.float32) * occ + rank
    first_rank = (round_s[0] * CAP).astype(jnp.float32)

    def joint_of(label):
        lane = lax.broadcasted_iota(jnp.int32, (1, 4 * slots), 1)
        row_of, slot_of = lax.div(lane, CAP), lax.rem(lane, CAP).astype(jnp.float32)
        irr_f = irr_v[...].astype(jnp.float32)
        goal = jnp.full((1, 4 * slots), -1.0, jnp.float32)
        start = jnp.full((1, 1), 0.0, jnp.float32) - (round_s[1] * JOINT).astype(jnp.float32)
        for row in range(4 * ROWS):
            want = (irr_s[z * 4 * ROWS + row] ^ label).astype(jnp.float32)
            fits = (irr_f == want) & (rank >= first_rank) & (rank < first_rank + CAP)
            size = jnp.sum(jnp.where(fits, 1.0, 0.0), axis=1, keepdims=True)
            goal = jnp.where((row_of == row) & (slot_of < size), start + slot_of, goal)
            start = start + size
        at = lax.broadcasted_iota(jnp.int32, (JOINT, 4 * slots), 0).astype(jnp.float32)
        return jnp.where(at == jnp.broadcast_to(goal, at.shape), 1.0, 0.0).astype(jnp.bfloat16)

    def targets(label, place):
        goal = place.astype(jnp.float32)
        for i in reversed(range(ROWS)):
            base = (irr_s[b * ROWS + i] ^ label) * occ + round_s[0] * CAP - CAP * i
            at = place.astype(jnp.float32) + base.astype(jnp.float32)
            goal = at if i == ROWS - 1 else jnp.where(place < CAP * (i + 1), at, goal)
        return goal

    key_b = jnp.broadcast_to(key, (slots, occ))
    sel = jnp.where(
        key_b == targets(my_label, lax.broadcasted_iota(jnp.int32, (slots, occ), 0)), 1.0, 0.0
    )
    coupling = jnp.where(equal, coup[...], 0.0)
    sel_c = product(sel, coupling, NT)
    for i in range(ROWS):
        rows = slice(CAP * i, CAP * i + CAP)
        pick = jnp.concatenate((sel[rows], sel_c[rows]), axis=0)
        packed = product(pick, amps[i], NN)
        lhs[plane, rows, 0:TILE] = packed[:CAP]
        lhs[plane, rows, TILE : 2 * TILE] = packed[CAP:]

    rows_to(plane, x_dev, 0).start()
    rows_to(plane, c_dev, 1).start()
    for kind in range(2):
        start_z(kind, 2)
    pack[...] = joint_of(my_label)
    for kind in range(2):
        start_z(kind, 3)
    from_x().wait_recv()
    rows_to(x_plane, x_dev, 0).wait_recv()
    rows_to(x_plane, c_dev, 2).start()
    rows_to(h * 2 + 1 - c, c_dev, 1).wait_recv()
    rows_to((1 - h) * 2 + 1 - c, c_dev, 2).wait_recv()
    hi, lo = split(lhs[...].reshape(4 * slots, 2 * TILE))
    lhs_hi[...] = jnp.dot(pack[...], hi, preferred_element_type=jnp.float32).astype(jnp.bfloat16)
    lhs_lo[...] = jnp.dot(pack[...], lo, preferred_element_type=jnp.float32).astype(jnp.bfloat16)

    def multiply(src):
        hi, lo = split(pan[src].reshape(64, 2 * TILE))
        value = lax.dot_general(hi, lhs_hi[...], NT, preferred_element_type=jnp.float32)
        value += lax.dot_general(hi, lhs_lo[...], NT, preferred_element_type=jnp.float32)
        value += lax.dot_general(lo, lhs_hi[...], NT, preferred_element_type=jnp.float32)
        part[src * 2] = value[:32]
        part[src * 2 + 1] = value[32:]

    multiply(z)
    for t in range(1, nz // 2 + 1):
        for kind in range(2):
            if t == 1 and nz // 2 >= 4:
                for more in range(4, nz // 2 + 1):
                    start_z(kind, more)
        for way in range(2):
            for kind in range(2):
                if t == reach[kind][way]:
                    got_z(kind, way, t).wait_recv()
        multiply(lax.rem(z + nz - t, nz))
        if 2 * t < nz:
            multiply(lax.rem(z + t, nz))

    def pair_copy(k):
        return remote(xs.at[k], xb.at[k], sem_x, (k,), x_pair)

    def y_copy(k):
        return remote(ys.at[k], yb.at[k], sem_y, (k,), y_dev(k))

    def owner(k):
        return lax.rem(y + k, ny) * 2

    order = []
    for far in range(ny // 2, 0, -1):
        order += [far] if 2 * far == ny else [far, ny - far]
    for k in order + [0]:
        xs[k] = part[order_s[owner(k) + 1 - xl]]
        pair_copy(k).start()
    for k in order:
        pair_copy(k).wait_recv()
        ys[k] = part[order_s[owner(k) + xl]] + xb[k]
        y_copy(k).start()
    out_label = pair_s[order_s[g]]
    pack[...] = joint_of(out_label)
    key_t = jnp.broadcast_to(key, (slots, occ)).T
    lane = lax.broadcasted_iota(jnp.int32, (occ, slots), 1)
    where = key_t == targets(out_label, lane)
    for i in range(ROWS):
        mine = where & (lane >= CAP * i) & (lane < CAP * (i + 1))
        place[occ * i : occ * (i + 1)] = jnp.where(mine, 1.0, 0.0).astype(jnp.bfloat16)
    pair_copy(0).wait_recv()
    total = part[order_s[g]] + xb[0]
    for k in order:
        y_copy(k).wait_recv()
        total += yb[k]
    hi, lo = split(total)
    total = jnp.dot(hi, pack[...], preferred_element_type=jnp.float32)
    total += jnp.dot(lo, pack[...], preferred_element_type=jnp.float32)

    quarter = c * 2 + h
    for r in range(4):
        res4[r] = total[:, slots * r : slots * (r + 1)]

    def plane_copy(d):
        to = lax.rem(plane + d, 4)
        return remote(res4.at[to], full.at[quarter], sem_f, (d,), {"blk": z * 4 + to})

    for d in range(1, 4):
        plane_copy(d).start()
    full[quarter] = res4[plane]

    for d in range(1, 4):
        other = lax.rem(plane + 4 - d, 4)
        other_quarter = lax.rem(other, 2) * 2 + lax.div(other, 2)
        remote(res4.at[0], full.at[other_quarter], sem_f, (d,), {"blk": c_dev}).wait_recv()
    hi, lo = split(full[...].reshape(TILE, slots).T)
    value = jnp.dot(place[...], hi, preferred_element_type=jnp.float32)
    value += jnp.dot(place[...], lo, preferred_element_type=jnp.float32)
    for i in range(ROWS):
        own[i] = value[occ * i : occ * (i + 1)]
        send[pl.ds(i, occ, stride=ROWS), :] = value[occ * i : occ * (i + 1)]

    def swap(d):
        to = lax.rem(b + d, nblk)
        return remote(
            send.at[pl.ds(pl.multiple_of(to * 16, 16), 16)],
            back.at[pl.ds(pl.multiple_of(b * 16, 16), 16)],
            sem_h,
            (d,),
            {"blk": to},
        )

    def start_swap(n, carry):
        odd = lax.rem(n, 2)
        half = lax.div(n, 2)
        swap(odd * (half + 1) + (1 - odd) * (nblk - half)).start()
        return carry

    lax.fori_loop(1, nblk, start_swap, 0)
    here = pl.ds(pl.multiple_of(b * 16, 16), 16)
    back[here] = send[here]

    irr_bi = irr_b.astype(jnp.int32)
    irr_ti = irr_t.astype(jnp.int32)
    plane_of = lax.broadcasted_iota(jnp.int32, (8, occ), 0) == lax.div(
        lax.broadcasted_iota(jnp.int32, (8, occ), 1), 4 * ROWS
    )
    plane_of = jnp.where(plane_of, 1.0, 0.0)
    worst = jnp.zeros((8, occ), jnp.float32)
    for label in range(8):
        hit = ((irr_bi ^ irr_ti) == label) & (rank < CAP)
        filled = jnp.dot(
            plane_of.astype(jnp.bfloat16),
            jnp.where(hit, 1.0, 0.0).astype(jnp.bfloat16),
            preferred_element_type=jnp.float32,
        )
        worst = jnp.maximum(worst, jnp.sum(filled, axis=1, keepdims=True))
    chunks = lax.div(jnp.max(worst).astype(jnp.int32) + JOINT - 1, JOINT)
    count_s[0] = lax.div(jnp.max(rank).astype(jnp.int32) + CAP, CAP) * chunks
    count_s[1] = chunks

    def take_swap(d, carry):
        src = lax.rem(b + nblk - d, nblk)
        remote(
            send.at[here], back.at[pl.ds(pl.multiple_of(src * 16, 16), 16)], sem_h, (d,), {"blk": c_dev}
        ).wait_recv()
        return carry

    lax.fori_loop(1, nblk, take_swap, 0)
    for j in range(ROWS):
        for i in range(ROWS):
            at = pl.ds(i, nblk, stride=ROWS)
            out[j, at, :] = own[j, at, :] - back[pl.ds(ROWS * j + i, nblk, stride=16), :]

    to_x().wait_send()
    rows_to(plane, x_dev, 0).wait_send()
    rows_to(plane, c_dev, 1).wait_send()
    rows_to(x_plane, c_dev, 2).wait_send()

    for kind in range(2):
        for way in range(2):
            for t in range(1, reach[kind][way] + 1):
                (to_x_z(way) if (kind, t) == (1, 1) else pass_z(kind, way, t)).wait_send()
    for k in order + [0]:
        pair_copy(k).wait_send()
    for k in order:
        y_copy(k).wait_send()
    for d in range(1, 4):
        plane_copy(d).wait_send()

    def end_swap(d, carry):
        swap(d).wait_send()
        return carry

    lax.fori_loop(1, nblk, end_swap, 0)


def shards(
    amplitudes, ladder_ints, cycle_ints, occ_coupling, occ_irrep, pair_irrep, screen, block_order
):
    rows, occ, tile = amplitudes.shape
    nz = lax.axis_size("blk") // 4
    ny = lax.axis_size("grp") // 2
    slots = ROWS * CAP
    f32 = jnp.float32
    smem = pl.BlockSpec(memory_space=pltpu.SMEM)
    vmem = pl.BlockSpec(memory_space=pltpu.VMEM)
    dma = pltpu.SemaphoreType.DMA
    call = pl.pallas_call(
        functools.partial(kernel, nz, ny),
        out_shape=(
            jax.ShapeDtypeStruct((rows, occ, tile), f32),
            jax.ShapeDtypeStruct((2,), jnp.int32),
        ),
        in_specs=[pl.BlockSpec(memory_space=pltpu.HBM)] * 10,
        out_specs=(vmem, smem),
        scratch_shapes=[
            pltpu.SMEM((3,), jnp.int32),
            pltpu.SMEM(occ_irrep.shape, jnp.int32),
            pltpu.SMEM(pair_irrep.shape, jnp.int32),
            pltpu.SMEM(screen.shape, jnp.int32),
            pltpu.SMEM(block_order.shape, jnp.int32),
            pltpu.VMEM((1, occ), jnp.int32),
            pltpu.VMEM((occ, occ), f32),
            pltpu.VMEM((rows, occ, tile), f32),
            pltpu.VMEM(ladder_ints.shape[::-1], f32),
            pltpu.VMEM(cycle_ints.shape[::-1], f32),
            pltpu.VMEM((2, 32, 2 * TILE), f32),
            pltpu.VMEM((nz, 2, 32, 2 * TILE), f32),
            pltpu.VMEM((4, slots, 2 * TILE), f32),
            pltpu.VMEM((JOINT, 2 * TILE), jnp.bfloat16),
            pltpu.VMEM((JOINT, 2 * TILE), jnp.bfloat16),
            pltpu.VMEM((JOINT, 4 * slots), jnp.bfloat16),
            pltpu.VMEM((rows * occ, slots), jnp.bfloat16),
            pltpu.VMEM((2 * nz, 32, JOINT), f32),
            pltpu.VMEM((ny, 32, JOINT), f32),
            pltpu.VMEM((ny, 32, JOINT), f32),
            pltpu.VMEM((ny, 32, JOINT), f32),
            pltpu.VMEM((ny, 32, JOINT), f32),
            pltpu.VMEM((4, 32, slots), f32),
            pltpu.VMEM((4, 32, slots), f32),
            pltpu.VMEM((rows, occ, tile), f32),
            pltpu.VMEM((rows * occ, tile), f32),
            pltpu.VMEM((rows * occ, tile), f32),
            dma((10,)),
            dma((2, 3)),
            dma((2, 1)),
            dma((2, 2, 2, nz // 2 + 1)),
            dma((2, ny)),
            dma((2, ny)),
            dma((2, 4)),
            dma((2, 4 * nz)),
        ],
        compiler_params=pltpu.CompilerParams(
            collective_id=0, has_side_effects=True, vmem_limit_bytes=24 << 20
        ),
    )

    def part(index):
        return call(
            index,
            occ_irrep, pair_irrep, screen, block_order, occ_irrep.reshape(1, occ),
            occ_coupling, amplitudes, ladder_ints.T, cycle_ints.T,
        )

    first, count = part(np.array((0, 0, 1), np.int32))

    def more(state):
        return state[0] < count[0]

    def again(state):
        index = jnp.stack((lax.div(state[0], count[1]), lax.rem(state[0], count[1]), jnp.int32(1)))
        return state[0] + 1, state[1] + part(index)[0]

    def rest(value):
        return lax.while_loop(more, again, (jnp.int32(1), value))[1]

    return lax.cond(count[0] > 1, rest, lambda value: value, first)


def solution(mesh):
    placed = (P("blk", None, "grp"), P("grp", "blk"), P("grp", "blk"), P(), P(), P(), P(), P())
    return jax.shard_map(
        shards, mesh=mesh, in_specs=placed, out_specs=P("blk", None, "grp"), check_vma=False
    )
```

```python
import functools

import jax
import jax.numpy as jnp
import numpy as np
from jax import lax
from jax.experimental import pallas as pl
from jax.experimental.pallas import tpu as pltpu
from jax.sharding import PartitionSpec as P

CAP = 32
JOINT = 384
ROWS = 4
TILE = 128
NT = (((1,), (1,)), ((), ()))
NN = (((1,), (0,)), ((), ()))


def split(x):
    hi = x.astype(jnp.bfloat16)
    return hi, (x - hi.astype(jnp.float32)).astype(jnp.bfloat16)


def product(a, b, dims):
    a_hi, a_lo = split(a)
    b_hi, b_lo = split(b)
    value = lax.dot_general(a_hi, b_hi, dims, preferred_element_type=jnp.float32)
    value += lax.dot_general(a_hi, b_lo, dims, preferred_element_type=jnp.float32)
    return value + lax.dot_general(a_lo, b_hi, dims, preferred_element_type=jnp.float32)


def kernel(
    nz, ny,
    *refs,
):
    given, (out, count_s), held = refs[:10], refs[10:12], refs[12:22]
    round_s, irr_s, pair_s, screen_s, order_s, irr_v, coup, amps, lad, cyc = held
    (
        psub, pan, lhs, lhs_hi, lhs_lo, pack, place, part, xs, xb, ys, yb, res4, full, own, send, back,
        sem_in, sem_a, sem_b, sem_c, sem_x, sem_y, sem_f, sem_h,
    ) = refs[22:]
    nblk = 4 * nz
    occ = amps.shape[1]
    slots = ROWS * CAP
    g = lax.axis_index("grp")
    b = lax.axis_index("blk")
    z = lax.div(b, 4)
    plane = lax.rem(b, 4)
    h = lax.div(plane, 2)
    c = lax.rem(plane, 2)
    y = lax.div(g, 2)
    xl = lax.rem(g, 2)
    x_dev = z * 4 + (1 - h) * 2 + c
    c_dev = z * 4 + h * 2 + (1 - c)
    x_plane = (1 - h) * 2 + c

    barrier = pltpu.get_barrier_semaphore()

    def greet(where):
        pl.semaphore_signal(barrier, inc=1, device_id=where, device_id_type=pl.DeviceIdType.MESH)

    def z_dev(d):
        return {"blk": lax.rem(z + nz + d, nz) * 4 + plane}

    def y_dev(d):
        return {"grp": lax.rem(y + ny + d, ny) * 2 + xl}

    x_pair = {"grp": y * 2 + 1 - xl}
    for d in range(1, 4):
        greet({"blk": z * 4 + lax.rem(plane + d, 4)})
    for d in (1, -1):
        greet(z_dev(d))
        greet({"blk": lax.rem(z + nz + d, nz) * 4 + x_plane})
    greet(x_pair)
    for d in range(1, ny):
        greet(y_dev(d))

    def fetch(n):
        return pltpu.make_async_copy(given[n], held[n], sem_in.at[n])

    for n in (8, 9, 2, 3, 1, 4, 0, 5, 6, 7):
        fetch(n).start()
    for n in (2, 3, 8, 9):
        fetch(n).wait()

    my_label = pair_s[g]
    tile_id = lax.div(b, 2)
    same = jnp.where(pair_s[tile_id] == my_label, 1.0, 0.0)
    kept = same * screen_s[g, tile_id].astype(jnp.float32)
    lad_t = lad[...] * kept
    cyc_t = cyc[...] * same
    for s in range(2):
        psub[s, :, 0:TILE] = lad_t[32 * s : 32 * s + 32]
        psub[s, :, TILE : 2 * TILE] = cyc_t[32 * s : 32 * s + 32]
    pan[z, h] = psub[h]

    pl.semaphore_wait(barrier, 8 + ny - 1)

    def remote(src, dst, sems, index, where):
        return pltpu.make_async_remote_copy(
            src_ref=src,
            dst_ref=dst,
            send_sem=sems.at[(0, *index)],
            recv_sem=sems.at[(1, *index)],
            device_id=where,
            device_id_type=pl.DeviceIdType.MESH,
        )

    def to_x():
        return remote(psub.at[1 - h], pan.at[z, h], sem_b, (0,), {"blk": x_dev})

    def from_x():
        return remote(psub.at[1 - h], pan.at[z, 1 - h], sem_b, (0,), {"blk": x_dev})

    def to_x_z(way):
        step = 1 - 2 * way
        return remote(
            psub.at[1 - h], pan.at[z, h], sem_c, (1, way, 1),
            {"blk": lax.rem(z + nz + step, nz) * 4 + x_plane},
        )

    tiles = (h, 1 - h)
    reach = ((nz // 2, nz - 1 - nz // 2), (nz - 1 - nz // 2, nz // 2))

    def pass_z(kind, way, t):
        step = 1 - 2 * way
        src = lax.rem(z + nz - step * (t - 1), nz)
        at = pan.at[src, tiles[kind]]
        return remote(at, at, sem_c, (kind, way, t), z_dev(step))

    def got_z(kind, way, t):
        step = 1 - 2 * way
        src = lax.rem(z + nz - step * t, nz)
        at = pan.at[src, tiles[kind]]
        return remote(at, at, sem_c, (kind, way, t), z_dev(step))

    def start_z(kind, t):
        for way in range(2):
            if t <= reach[kind][way]:
                if t > 1:
                    got_z(kind, way, t - 1).wait_recv()
                pass_z(kind, way, t).start()

    def rows_to(src, where, k):
        return remote(lhs.at[src], lhs.at[src], sem_a, (k,), {"blk": where})

    to_x().start()
    for way in range(2):
        if reach[1][way]:
            to_x_z(way).start()
    start_z(0, 1)
    for n in (0, 1, 4, 5, 6, 7):
        fetch(n).wait()

    irr_b = jnp.broadcast_to(irr_v[...].astype(jnp.float32), (occ, occ))
    irr_t = irr_b.T
    equal = irr_b == irr_t
    before = lax.broadcasted_iota(jnp.int32, (occ, occ), 0) < lax.broadcasted_iota(
        jnp.int32, (occ, occ), 1
    )
    rank = jnp.sum(jnp.where(equal & before, 1.0, 0.0), axis=0, keepdims=True)
    key = irr_v[...].astype(jnp.float32) * occ + rank
    first_rank = (round_s[0] * CAP).astype(jnp.float32)

    def joint_of(label):
        lane = lax.broadcasted_iota(jnp.int32, (1, 4 * slots), 1)
        row_of, slot_of = lax.div(lane, CAP), lax.rem(lane, CAP).astype(jnp.float32)
        irr_f = irr_v[...].astype(jnp.float32)
        goal = jnp.full((1, 4 * slots), -1.0, jnp.float32)
        start = jnp.full((1, 1), 0.0, jnp.float32) - (round_s[1] * JOINT).astype(jnp.float32)
        for row in range(4 * ROWS):
            want = (irr_s[z * 4 * ROWS + row] ^ label).astype(jnp.float32)
            fits = (irr_f == want) & (rank >= first_rank) & (rank < first_rank + CAP)
            size = jnp.sum(jnp.where(fits, 1.0, 0.0), axis=1, keepdims=True)
            goal = jnp.where((row_of == row) & (slot_of < size), start + slot_of, goal)
            start = start + size
        at = lax.broadcasted_iota(jnp.int32, (JOINT, 4 * slots), 0).astype(jnp.float32)
        return jnp.where(at == jnp.broadcast_to(goal, at.shape), 1.0, 0.0).astype(jnp.bfloat16)

    def targets(label, place):
        goal = place.astype(jnp.float32)
        for i in reversed(range(ROWS)):
            base = (irr_s[b * ROWS + i] ^ label) * occ + round_s[0] * CAP - CAP * i
            at = place.astype(jnp.float32) + base.astype(jnp.float32)
            goal = at if i == ROWS - 1 else jnp.where(place < CAP * (i + 1), at, goal)
        return goal

    key_b = jnp.broadcast_to(key, (slots, occ))
    sel = jnp.where(
        key_b == targets(my_label, lax.broadcasted_iota(jnp.int32, (slots, occ), 0)), 1.0, 0.0
    )
    coupling = jnp.where(equal, coup[...], 0.0)
    sel_c = product(sel, coupling, NT)
    for i in range(ROWS):
        rows = slice(CAP * i, CAP * i + CAP)
        pick = jnp.concatenate((sel[rows], sel_c[rows]), axis=0)
        packed = product(pick, amps[i], NN)
        lhs[plane, rows, 0:TILE] = packed[:CAP]
        lhs[plane, rows, TILE : 2 * TILE] = packed[CAP:]

    rows_to(plane, x_dev, 0).start()
    rows_to(plane, c_dev, 1).start()
    for kind in range(2):
        start_z(kind, 2)
    pack[...] = joint_of(my_label)
    for kind in range(2):
        start_z(kind, 3)
    from_x().wait_recv()
    rows_to(x_plane, x_dev, 0).wait_recv()
    rows_to(x_plane, c_dev, 2).start()
    for kind in range(2):
        for t in range(4, nz // 2 + 1):
            start_z(kind, t)
    rows_to(h * 2 + 1 - c, c_dev, 1).wait_recv()
    rows_to((1 - h) * 2 + 1 - c, c_dev, 2).wait_recv()
    hi, lo = split(lhs[...].reshape(4 * slots, 2 * TILE))
    lhs_hi[...] = jnp.dot(pack[...], hi, preferred_element_type=jnp.float32).astype(jnp.bfloat16)
    lhs_lo[...] = jnp.dot(pack[...], lo, preferred_element_type=jnp.float32).astype(jnp.bfloat16)

    def multiply(src):
        hi, lo = split(pan[src].reshape(64, 2 * TILE))
        value = lax.dot_general(hi, lhs_hi[...], NT, preferred_element_type=jnp.float32)
        value += lax.dot_general(hi, lhs_lo[...], NT, preferred_element_type=jnp.float32)
        value += lax.dot_general(lo, lhs_hi[...], NT, preferred_element_type=jnp.float32)
        part[src * 2] = value[:32]
        part[src * 2 + 1] = value[32:]

    multiply(z)
    for t in range(1, nz // 2 + 1):
        for way in range(2):
            for kind in range(2):
                if t == reach[kind][way]:
                    got_z(kind, way, t).wait_recv()
        multiply(lax.rem(z + nz - t, nz))
        if 2 * t < nz:
            multiply(lax.rem(z + t, nz))

    def pair_copy(k):
        return remote(xs.at[k], xb.at[k], sem_x, (k,), x_pair)

    def y_copy(k):
        return remote(ys.at[k], yb.at[k], sem_y, (k,), y_dev(k))

    def owner(k):
        return lax.rem(y + k, ny) * 2

    order = []
    for far in range(ny // 2, 0, -1):
        order += [far] if 2 * far == ny else [far, ny - far]
    for k in order + [0]:
        xs[k] = part[order_s[owner(k) + 1 - xl]]
        pair_copy(k).start()
    for k in order:
        pair_copy(k).wait_recv()
        ys[k] = part[order_s[owner(k) + xl]] + xb[k]
        y_copy(k).start()
    out_label = pair_s[order_s[g]]
    pack[...] = joint_of(out_label)
    key_t = jnp.broadcast_to(key, (slots, occ)).T
    lane = lax.broadcasted_iota(jnp.int32, (occ, slots), 1)
    where = key_t == targets(out_label, lane)
    for i in range(ROWS):
        mine = where & (lane >= CAP * i) & (lane < CAP * (i + 1))
        place[occ * i : occ * (i + 1)] = jnp.where(mine, 1.0, 0.0).astype(jnp.bfloat16)
    pair_copy(0).wait_recv()
    total = part[order_s[g]] + xb[0]
    for k in order:
        y_copy(k).wait_recv()
        total += yb[k]
    hi, lo = split(total)
    total = jnp.dot(hi, pack[...], preferred_element_type=jnp.float32)
    total += jnp.dot(lo, pack[...], preferred_element_type=jnp.float32)

    quarter = c * 2 + h
    for r in range(4):
        res4[r] = total[:, slots * r : slots * (r + 1)]

    def plane_copy(d):
        to = lax.rem(plane + d, 4)
        return remote(res4.at[to], full.at[quarter], sem_f, (d,), {"blk": z * 4 + to})

    for d in range(1, 4):
        plane_copy(d).start()
    full[quarter] = res4[plane]

    for d in range(1, 4):
        other = lax.rem(plane + 4 - d, 4)
        other_quarter = lax.rem(other, 2) * 2 + lax.div(other, 2)
        remote(res4.at[0], full.at[other_quarter], sem_f, (d,), {"blk": c_dev}).wait_recv()
    hi, lo = split(full[...].reshape(TILE, slots).T)
    value = jnp.dot(place[...], hi, preferred_element_type=jnp.float32)
    value += jnp.dot(place[...], lo, preferred_element_type=jnp.float32)
    for i in range(ROWS):
        own[i] = value[occ * i : occ * (i + 1)]
        send[pl.ds(i, occ, stride=ROWS), :] = value[occ * i : occ * (i + 1)]

    def swap(d):
        to = lax.rem(b + d, nblk)
        return remote(
            send.at[pl.ds(pl.multiple_of(to * 16, 16), 16)],
            back.at[pl.ds(pl.multiple_of(b * 16, 16), 16)],
            sem_h,
            (0,),
            {"blk": to},
        )

    def all_swaps():
        most = pl.ds(0, 16 * (nblk - 1))
        return remote(send.at[most], back.at[most], sem_h, (0,), {"blk": c_dev})

    def start_swap(m, carry):
        n = nblk - m
        odd = lax.rem(n, 2)
        half = lax.div(n, 2)
        swap(odd * (half + 1) + (1 - odd) * (nblk - half)).start()
        return carry

    lax.fori_loop(1, nblk, start_swap, 0)
    here = pl.ds(pl.multiple_of(b * 16, 16), 16)
    back[here] = send[here]

    irr_bi = irr_b.astype(jnp.int32)
    irr_ti = irr_t.astype(jnp.int32)
    plane_of = lax.broadcasted_iota(jnp.int32, (8, occ), 0) == lax.div(
        lax.broadcasted_iota(jnp.int32, (8, occ), 1), 4 * ROWS
    )
    plane_of = jnp.where(plane_of, 1.0, 0.0)
    worst = jnp.zeros((8, occ), jnp.float32)
    for label in range(8):
        hit = ((irr_bi ^ irr_ti) == label) & (rank < CAP)
        filled = jnp.dot(
            plane_of.astype(jnp.bfloat16),
            jnp.where(hit, 1.0, 0.0).astype(jnp.bfloat16),
            preferred_element_type=jnp.float32,
        )
        worst = jnp.maximum(worst, jnp.sum(filled, axis=1, keepdims=True))
    chunks = lax.div(jnp.max(worst).astype(jnp.int32) + JOINT - 1, JOINT)
    count_s[0] = lax.div(jnp.max(rank).astype(jnp.int32) + CAP, CAP) * chunks
    count_s[1] = chunks

    to_x().wait_send()
    rows_to(plane, x_dev, 0).wait_send()
    rows_to(plane, c_dev, 1).wait_send()
    rows_to(x_plane, c_dev, 2).wait_send()

    for kind in range(2):
        for way in range(2):
            for t in range(1, reach[kind][way] + 1):
                (to_x_z(way) if (kind, t) == (1, 1) else pass_z(kind, way, t)).wait_send()
    for k in order + [0]:
        pair_copy(k).wait_send()
    for k in order:
        y_copy(k).wait_send()
    for d in range(1, 4):
        plane_copy(d).wait_send()
    all_swaps().wait_recv()
    for j in range(ROWS):
        for i in range(ROWS):
            at = pl.ds(i, nblk, stride=ROWS)
            out[j, at, :] = own[j, at, :] - back[pl.ds(ROWS * j + i, nblk, stride=16), :]

    all_swaps().wait_send()


def shards(
    amplitudes, ladder_ints, cycle_ints, occ_coupling, occ_irrep, pair_irrep, screen, block_order
):
    rows, occ, tile = amplitudes.shape
    nz = lax.axis_size("blk") // 4
    ny = lax.axis_size("grp") // 2
    slots = ROWS * CAP
    f32 = jnp.float32
    smem = pl.BlockSpec(memory_space=pltpu.SMEM)
    vmem = pl.BlockSpec(memory_space=pltpu.VMEM)
    dma = pltpu.SemaphoreType.DMA
    call = pl.pallas_call(
        functools.partial(kernel, nz, ny),
        out_shape=(
            jax.ShapeDtypeStruct((rows, occ, tile), f32),
            jax.ShapeDtypeStruct((2,), jnp.int32),
        ),
        in_specs=[pl.BlockSpec(memory_space=pltpu.HBM)] * 10,
        out_specs=(vmem, smem),
        scratch_shapes=[
            pltpu.SMEM((3,), jnp.int32),
            pltpu.SMEM(occ_irrep.shape, jnp.int32),
            pltpu.SMEM(pair_irrep.shape, jnp.int32),
            pltpu.SMEM(screen.shape, jnp.int32),
            pltpu.SMEM(block_order.shape, jnp.int32),
            pltpu.VMEM((1, occ), jnp.int32),
            pltpu.VMEM((occ, occ), f32),
            pltpu.VMEM((rows, occ, tile), f32),
            pltpu.VMEM(ladder_ints.shape[::-1], f32),
            pltpu.VMEM(cycle_ints.shape[::-1], f32),
            pltpu.VMEM((2, 32, 2 * TILE), f32),
            pltpu.VMEM((nz, 2, 32, 2 * TILE), f32),
            pltpu.VMEM((4, slots, 2 * TILE), f32),
            pltpu.VMEM((JOINT, 2 * TILE), jnp.bfloat16),
            pltpu.VMEM((JOINT, 2 * TILE), jnp.bfloat16),
            pltpu.VMEM((JOINT, 4 * slots), jnp.bfloat16),
            pltpu.VMEM((rows * occ, slots), jnp.bfloat16),
            pltpu.VMEM((2 * nz, 32, JOINT), f32),
            pltpu.VMEM((ny, 32, JOINT), f32),
            pltpu.VMEM((ny, 32, JOINT), f32),
            pltpu.VMEM((ny, 32, JOINT), f32),
            pltpu.VMEM((ny, 32, JOINT), f32),
            pltpu.VMEM((4, 32, slots), f32),
            pltpu.VMEM((4, 32, slots), f32),
            pltpu.VMEM((rows, occ, tile), f32),
            pltpu.VMEM((rows * occ, tile), f32),
            pltpu.VMEM((rows * occ, tile), f32),
            dma((10,)),
            dma((2, 3)),
            dma((2, 1)),
            dma((2, 2, 2, nz // 2 + 1)),
            dma((2, ny)),
            dma((2, ny)),
            dma((2, 4)),
            dma((2, 1)),
        ],
        compiler_params=pltpu.CompilerParams(
            collective_id=0, has_side_effects=True, vmem_limit_bytes=24 << 20
        ),
    )

    def part(index):
        return call(
            index,
            occ_irrep, pair_irrep, screen, block_order, occ_irrep.reshape(1, occ),
            occ_coupling, amplitudes, ladder_ints.T, cycle_ints.T,
        )

    first, count = part(np.array((0, 0, 1), np.int32))

    def more(state):
        return state[0] < count[0]

    def again(state):
        index = jnp.stack((lax.div(state[0], count[1]), lax.rem(state[0], count[1]), jnp.int32(1)))
        return state[0] + 1, state[1] + part(index)[0]

    def rest(value):
        return lax.while_loop(more, again, (jnp.int32(1), value))[1]

    return lax.cond(count[0] > 1, rest, lambda value: value, first)


def solution(mesh):
    placed = (P("blk", None, "grp"), P("grp", "blk"), P("grp", "blk"), P(), P(), P(), P(), P())
    return jax.shard_map(
        shards, mesh=mesh, in_specs=placed, out_specs=P("blk", None, "grp"), check_vma=False
    )
```

```python
import functools

import jax
import jax.numpy as jnp
import numpy as np
from jax import lax
from jax.experimental import pallas as pl
from jax.experimental.pallas import tpu as pltpu
from jax.sharding import PartitionSpec as P

CAP = 32
JOINT = 384
ROWS = 4
TILE = 128
NT = (((1,), (1,)), ((), ()))
NN = (((1,), (0,)), ((), ()))


def split(x):
    hi = x.astype(jnp.bfloat16)
    return hi, (x - hi.astype(jnp.float32)).astype(jnp.bfloat16)


def product(a, b, dims):
    a_hi, a_lo = split(a)
    b_hi, b_lo = split(b)
    value = lax.dot_general(a_hi, b_hi, dims, preferred_element_type=jnp.float32)
    value += lax.dot_general(a_hi, b_lo, dims, preferred_element_type=jnp.float32)
    return value + lax.dot_general(a_lo, b_hi, dims, preferred_element_type=jnp.float32)


def kernel(
    nz, ny,
    *refs,
):
    given, (out, count_s), held = refs[:10], refs[10:12], refs[12:22]
    round_s, irr_s, pair_s, screen_s, order_s, irr_v, coup, amps, lad, cyc = held
    (
        psub, pan, lhs, lhs_hi, lhs_lo, pack, place, part, xs, xb, ys, yb, res4, full, own, send, back,
        sem_in, sem_a, sem_b, sem_c, sem_x, sem_y, sem_f, sem_h,
    ) = refs[22:]
    nblk = 4 * nz
    occ = amps.shape[1]
    slots = ROWS * CAP
    g = lax.axis_index("grp")
    b = lax.axis_index("blk")
    z = lax.div(b, 4)
    plane = lax.rem(b, 4)
    h = lax.div(plane, 2)
    c = lax.rem(plane, 2)
    y = lax.div(g, 2)
    xl = lax.rem(g, 2)
    x_dev = z * 4 + (1 - h) * 2 + c
    c_dev = z * 4 + h * 2 + (1 - c)
    x_plane = (1 - h) * 2 + c

    barrier = pltpu.get_barrier_semaphore()

    def greet(where):
        pl.semaphore_signal(barrier, inc=1, device_id=where, device_id_type=pl.DeviceIdType.MESH)

    def z_dev(d):
        return {"blk": lax.rem(z + nz + d, nz) * 4 + plane}

    def y_dev(d):
        return {"grp": lax.rem(y + ny + d, ny) * 2 + xl}

    x_pair = {"grp": y * 2 + 1 - xl}
    for d in (1, -1):
        greet(z_dev(d))
        greet({"blk": lax.rem(z + nz + d, nz) * 4 + x_plane})
    for d in range(1, 4):
        greet({"blk": z * 4 + lax.rem(plane + d, 4)})
    greet(x_pair)
    for d in range(1, ny):
        greet(y_dev(d))

    def fetch(n):
        return pltpu.make_async_copy(given[n], held[n], sem_in.at[n])

    for n in (8, 9, 2, 3, 1, 4, 0, 5, 6, 7):
        fetch(n).start()
    for n in (2, 3, 8, 9):
        fetch(n).wait()

    my_label = pair_s[g]
    tile_id = lax.div(b, 2)
    same = jnp.where(pair_s[tile_id] == my_label, 1.0, 0.0)
    kept = same * screen_s[g, tile_id].astype(jnp.float32)
    lad_t = lad[...] * kept
    cyc_t = cyc[...] * same
    for s in range(2):
        psub[s, :, 0:TILE] = lad_t[32 * s : 32 * s + 32]
        psub[s, :, TILE : 2 * TILE] = cyc_t[32 * s : 32 * s + 32]
    pan[z, h] = psub[h]

    pl.semaphore_wait(barrier, 8 + ny - 1)

    def remote(src, dst, sems, index, where):
        return pltpu.make_async_remote_copy(
            src_ref=src,
            dst_ref=dst,
            send_sem=sems.at[(0, *index)],
            recv_sem=sems.at[(1, *index)],
            device_id=where,
            device_id_type=pl.DeviceIdType.MESH,
        )

    def to_x():
        return remote(psub.at[1 - h], pan.at[z, h], sem_b, (0,), {"blk": x_dev})

    def from_x():
        return remote(psub.at[1 - h], pan.at[z, 1 - h], sem_b, (0,), {"blk": x_dev})

    def to_x_z(way):
        step = 1 - 2 * way
        return remote(
            psub.at[1 - h], pan.at[z, h], sem_c, (1, way, 1),
            {"blk": lax.rem(z + nz + step, nz) * 4 + x_plane},
        )

    tiles = (h, 1 - h)
    reach = ((nz // 2, nz - 1 - nz // 2), (nz - 1 - nz // 2, nz // 2))

    def pass_z(kind, way, t):
        step = 1 - 2 * way
        src = lax.rem(z + nz - step * (t - 1), nz)
        at = pan.at[src, tiles[kind]]
        return remote(at, at, sem_c, (kind, way, t), z_dev(step))

    def got_z(kind, way, t):
        step = 1 - 2 * way
        src = lax.rem(z + nz - step * t, nz)
        at = pan.at[src, tiles[kind]]
        return remote(at, at, sem_c, (kind, way, t), z_dev(step))

    def start_z(kind, t):
        for way in range(2):
            if t <= reach[kind][way]:
                if t > 1:
                    got_z(kind, way, t - 1).wait_recv()
                pass_z(kind, way, t).start()

    def rows_to(src, where, k):
        return remote(lhs.at[src], lhs.at[src], sem_a, (k,), {"blk": where})

    to_x().start()
    for way in range(2):
        if reach[1][way]:
            to_x_z(way).start()
    start_z(0, 1)
    for n in (0, 1, 4, 5, 6, 7):
        fetch(n).wait()

    irr_b = jnp.broadcast_to(irr_v[...].astype(jnp.float32), (occ, occ))
    irr_t = irr_b.T
    equal = irr_b == irr_t
    before = lax.broadcasted_iota(jnp.int32, (occ, occ), 0) < lax.broadcasted_iota(
        jnp.int32, (occ, occ), 1
    )
    rank = jnp.sum(jnp.where(equal & before, 1.0, 0.0), axis=0, keepdims=True)
    key = irr_v[...].astype(jnp.float32) * occ + rank
    first_rank = (round_s[0] * CAP).astype(jnp.float32)

    def joint_of(label):
        lane = lax.broadcasted_iota(jnp.int32, (1, 4 * slots), 1)
        row_of, slot_of = lax.div(lane, CAP), lax.rem(lane, CAP).astype(jnp.float32)
        irr_f = irr_v[...].astype(jnp.float32)
        goal = jnp.full((1, 4 * slots), -1.0, jnp.float32)
        start = jnp.full((1, 1), 0.0, jnp.float32) - (round_s[1] * JOINT).astype(jnp.float32)
        for row in range(4 * ROWS):
            want = (irr_s[z * 4 * ROWS + row] ^ label).astype(jnp.float32)
            fits = (irr_f == want) & (rank >= first_rank) & (rank < first_rank + CAP)
            size = jnp.sum(jnp.where(fits, 1.0, 0.0), axis=1, keepdims=True)
            goal = jnp.where((row_of == row) & (slot_of < size), start + slot_of, goal)
            start = start + size
        at = lax.broadcasted_iota(jnp.int32, (JOINT, 4 * slots), 0).astype(jnp.float32)
        return jnp.where(at == jnp.broadcast_to(goal, at.shape), 1.0, 0.0).astype(jnp.bfloat16)

    def targets(label, place):
        goal = place.astype(jnp.float32)
        for i in reversed(range(ROWS)):
            base = (irr_s[b * ROWS + i] ^ label) * occ + round_s[0] * CAP - CAP * i
            at = place.astype(jnp.float32) + base.astype(jnp.float32)
            goal = at if i == ROWS - 1 else jnp.where(place < CAP * (i + 1), at, goal)
        return goal

    key_b = jnp.broadcast_to(key, (slots, occ))
    sel = jnp.where(
        key_b == targets(my_label, lax.broadcasted_iota(jnp.int32, (slots, occ), 0)), 1.0, 0.0
    )
    coupling = jnp.where(equal, coup[...], 0.0)
    sel_c = product(sel, coupling, NT)
    for i in range(ROWS):
        rows = slice(CAP * i, CAP * i + CAP)
        pick = jnp.concatenate((sel[rows], sel_c[rows]), axis=0)
        packed = product(pick, amps[i], NN)
        lhs[plane, rows, 0:TILE] = packed[:CAP]
        lhs[plane, rows, TILE : 2 * TILE] = packed[CAP:]

    rows_to(plane, x_dev, 0).start()
    rows_to(plane, c_dev, 1).start()
    for kind in range(2):
        start_z(kind, 2)
    pack[...] = joint_of(my_label)
    for kind in range(2):
        start_z(kind, 3)
    from_x().wait_recv()
    rows_to(x_plane, x_dev, 0).wait_recv()
    rows_to(x_plane, c_dev, 2).start()
    for kind in range(2):
        for t in range(4, nz // 2 + 1):
            start_z(kind, t)
    rows_to(h * 2 + 1 - c, c_dev, 1).wait_recv()
    rows_to((1 - h) * 2 + 1 - c, c_dev, 2).wait_recv()
    hi, lo = split(lhs[...].reshape(4 * slots, 2 * TILE))
    lhs_hi[...] = jnp.dot(pack[...], hi, preferred_element_type=jnp.float32).astype(jnp.bfloat16)
    lhs_lo[...] = jnp.dot(pack[...], lo, preferred_element_type=jnp.float32).astype(jnp.bfloat16)

    def multiply(src):
        hi, lo = split(pan[src].reshape(64, 2 * TILE))
        value = lax.dot_general(hi, lhs_hi[...], NT, preferred_element_type=jnp.float32)
        value += lax.dot_general(hi, lhs_lo[...], NT, preferred_element_type=jnp.float32)
        value += lax.dot_general(lo, lhs_hi[...], NT, preferred_element_type=jnp.float32)
        part[src * 2] = value[:32]
        part[src * 2 + 1] = value[32:]

    multiply(z)
    for t in range(1, nz // 2 + 1):
        for way in range(2):
            for kind in range(2):
                if t == reach[kind][way]:
                    got_z(kind, way, t).wait_recv()
        multiply(lax.rem(z + nz - t, nz))
        if 2 * t < nz:
            multiply(lax.rem(z + t, nz))

    def pair_copy(k):
        return remote(xs.at[k], xb.at[k], sem_x, (k,), x_pair)

    def y_copy(k):
        return remote(ys.at[k], yb.at[k], sem_y, (k,), y_dev(k))

    def owner(k):
        return lax.rem(y + k, ny) * 2

    order = []
    for far in range(ny // 2, 0, -1):
        order += [far] if 2 * far == ny else [far, ny - far]
    for k in order + [0]:
        xs[k] = part[order_s[owner(k) + 1 - xl]]
        pair_copy(k).start()
    for k in order:
        pair_copy(k).wait_recv()
        ys[k] = part[order_s[owner(k) + xl]] + xb[k]
        y_copy(k).start()
    out_label = pair_s[order_s[g]]
    pack[...] = joint_of(out_label)
    key_t = jnp.broadcast_to(key, (slots, occ)).T
    lane = lax.broadcasted_iota(jnp.int32, (occ, slots), 1)
    where = key_t == targets(out_label, lane)
    for i in range(ROWS):
        mine = where & (lane >= CAP * i) & (lane < CAP * (i + 1))
        place[occ * i : occ * (i + 1)] = jnp.where(mine, 1.0, 0.0).astype(jnp.bfloat16)
    pair_copy(0).wait_recv()
    total = part[order_s[g]] + xb[0]
    for k in order:
        y_copy(k).wait_recv()
        total += yb[k]
    hi, lo = split(total)
    total = jnp.dot(hi, pack[...], preferred_element_type=jnp.float32)
    total += jnp.dot(lo, pack[...], preferred_element_type=jnp.float32)

    quarter = c * 2 + h
    for r in range(4):
        res4[r] = total[:, slots * r : slots * (r + 1)]

    def plane_copy(d):
        to = lax.rem(plane + d, 4)
        return remote(res4.at[to], full.at[quarter], sem_f, (d,), {"blk": z * 4 + to})

    for d in range(1, 4):
        plane_copy(d).start()
    full[quarter] = res4[plane]

    for d in range(1, 4):
        other = lax.rem(plane + 4 - d, 4)
        other_quarter = lax.rem(other, 2) * 2 + lax.div(other, 2)
        remote(res4.at[0], full.at[other_quarter], sem_f, (d,), {"blk": c_dev}).wait_recv()
    hi, lo = split(full[...].reshape(TILE, slots).T)
    value = jnp.dot(place[...], hi, preferred_element_type=jnp.float32)
    value += jnp.dot(place[...], lo, preferred_element_type=jnp.float32)
    for i in range(ROWS):
        own[i] = value[occ * i : occ * (i + 1)]
        send[pl.ds(i, occ, stride=ROWS), :] = value[occ * i : occ * (i + 1)]

    def swap(d):
        to = lax.rem(b + d, nblk)
        return remote(
            send.at[pl.ds(pl.multiple_of(to * 16, 16), 16)],
            back.at[pl.ds(pl.multiple_of(b * 16, 16), 16)],
            sem_h,
            (0,),
            {"blk": to},
        )

    def all_swaps():
        most = pl.ds(0, 16 * (nblk - 1))
        return remote(send.at[most], back.at[most], sem_h, (0,), {"blk": c_dev})

    def start_swap(m, carry):
        n = nblk - m
        odd = lax.rem(n, 2)
        half = lax.div(n, 2)
        swap(odd * (half + 1) + (1 - odd) * (nblk - half)).start()
        return carry

    lax.fori_loop(1, nblk, start_swap, 0)
    here = pl.ds(pl.multiple_of(b * 16, 16), 16)
    back[here] = send[here]

    irr_bi = irr_b.astype(jnp.int32)
    irr_ti = irr_t.astype(jnp.int32)
    plane_of = lax.broadcasted_iota(jnp.int32, (8, occ), 0) == lax.div(
        lax.broadcasted_iota(jnp.int32, (8, occ), 1), 4 * ROWS
    )
    plane_of = jnp.where(plane_of, 1.0, 0.0)
    worst = jnp.zeros((8, occ), jnp.float32)
    for label in range(8):
        hit = ((irr_bi ^ irr_ti) == label) & (rank < CAP)
        filled = jnp.dot(
            plane_of.astype(jnp.bfloat16),
            jnp.where(hit, 1.0, 0.0).astype(jnp.bfloat16),
            preferred_element_type=jnp.float32,
        )
        worst = jnp.maximum(worst, jnp.sum(filled, axis=1, keepdims=True))
    chunks = lax.div(jnp.max(worst).astype(jnp.int32) + JOINT - 1, JOINT)
    count_s[0] = lax.div(jnp.max(rank).astype(jnp.int32) + CAP, CAP) * chunks
    count_s[1] = chunks

    to_x().wait_send()
    rows_to(plane, x_dev, 0).wait_send()
    rows_to(plane, c_dev, 1).wait_send()
    rows_to(x_plane, c_dev, 2).wait_send()

    for kind in range(2):
        for way in range(2):
            for t in range(1, reach[kind][way] + 1):
                (to_x_z(way) if (kind, t) == (1, 1) else pass_z(kind, way, t)).wait_send()
    for k in order + [0]:
        pair_copy(k).wait_send()
    for k in order:
        y_copy(k).wait_send()
    for d in range(1, 4):
        plane_copy(d).wait_send()
    all_swaps().wait_recv()
    for j in range(ROWS):
        for i in range(ROWS):
            at = pl.ds(i, nblk, stride=ROWS)
            out[j, at, :] = own[j, at, :] - back[pl.ds(ROWS * j + i, nblk, stride=16), :]

    all_swaps().wait_send()


def shards(
    amplitudes, ladder_ints, cycle_ints, occ_coupling, occ_irrep, pair_irrep, screen, block_order
):
    rows, occ, tile = amplitudes.shape
    nz = lax.axis_size("blk") // 4
    ny = lax.axis_size("grp") // 2
    slots = ROWS * CAP
    f32 = jnp.float32
    smem = pl.BlockSpec(memory_space=pltpu.SMEM)
    vmem = pl.BlockSpec(memory_space=pltpu.VMEM)
    dma = pltpu.SemaphoreType.DMA
    call = pl.pallas_call(
        functools.partial(kernel, nz, ny),
        out_shape=(
            jax.ShapeDtypeStruct((rows, occ, tile), f32),
            jax.ShapeDtypeStruct((2,), jnp.int32),
        ),
        in_specs=[pl.BlockSpec(memory_space=pltpu.HBM)] * 10,
        out_specs=(vmem, smem),
        scratch_shapes=[
            pltpu.SMEM((3,), jnp.int32),
            pltpu.SMEM(occ_irrep.shape, jnp.int32),
            pltpu.SMEM(pair_irrep.shape, jnp.int32),
            pltpu.SMEM(screen.shape, jnp.int32),
            pltpu.SMEM(block_order.shape, jnp.int32),
            pltpu.VMEM((1, occ), jnp.int32),
            pltpu.VMEM((occ, occ), f32),
            pltpu.VMEM((rows, occ, tile), f32),
            pltpu.VMEM(ladder_ints.shape[::-1], f32),
            pltpu.VMEM(cycle_ints.shape[::-1], f32),
            pltpu.VMEM((2, 32, 2 * TILE), f32),
            pltpu.VMEM((nz, 2, 32, 2 * TILE), f32),
            pltpu.VMEM((4, slots, 2 * TILE), f32),
            pltpu.VMEM((JOINT, 2 * TILE), jnp.bfloat16),
            pltpu.VMEM((JOINT, 2 * TILE), jnp.bfloat16),
            pltpu.VMEM((JOINT, 4 * slots), jnp.bfloat16),
            pltpu.VMEM((rows * occ, slots), jnp.bfloat16),
            pltpu.VMEM((2 * nz, 32, JOINT), f32),
            pltpu.VMEM((ny, 32, JOINT), f32),
            pltpu.VMEM((ny, 32, JOINT), f32),
            pltpu.VMEM((ny, 32, JOINT), f32),
            pltpu.VMEM((ny, 32, JOINT), f32),
            pltpu.VMEM((4, 32, slots), f32),
            pltpu.VMEM((4, 32, slots), f32),
            pltpu.VMEM((rows, occ, tile), f32),
            pltpu.VMEM((rows * occ, tile), f32),
            pltpu.VMEM((rows * occ, tile), f32),
            dma((10,)),
            dma((2, 3)),
            dma((2, 1)),
            dma((2, 2, 2, nz // 2 + 1)),
            dma((2, ny)),
            dma((2, ny)),
            dma((2, 4)),
            dma((2, 1)),
        ],
        compiler_params=pltpu.CompilerParams(
            collective_id=0, has_side_effects=True, vmem_limit_bytes=24 << 20
        ),
    )

    def part(index):
        return call(
            index,
            occ_irrep, pair_irrep, screen, block_order, occ_irrep.reshape(1, occ),
            occ_coupling, amplitudes, ladder_ints.T, cycle_ints.T,
        )

    first, count = part(np.array((0, 0, 1), np.int32))

    def more(state):
        return state[0] < count[0]

    def again(state):
        index = jnp.stack((lax.div(state[0], count[1]), lax.rem(state[0], count[1]), jnp.int32(1)))
        return state[0] + 1, state[1] + part(index)[0]

    def rest(value):
        return lax.while_loop(more, again, (jnp.int32(1), value))[1]

    return lax.cond(count[0] > 1, rest, lambda value: value, first)


def solution(mesh):
    placed = (P("blk", None, "grp"), P("grp", "blk"), P("grp", "blk"), P(), P(), P(), P(), P())
    return jax.shard_map(
        shards, mesh=mesh, in_specs=placed, out_specs=P("blk", None, "grp"), check_vma=False
    )
```

```python
import functools

import jax
import jax.numpy as jnp
import numpy as np
from jax import lax
from jax.experimental import pallas as pl
from jax.experimental.pallas import tpu as pltpu
from jax.sharding import PartitionSpec as P

CAP = 32
JOINT = 384
ROWS = 4
TILE = 128
NT = (((1,), (1,)), ((), ()))
NN = (((1,), (0,)), ((), ()))


def split(x):
    hi = x.astype(jnp.bfloat16)
    return hi, (x - hi.astype(jnp.float32)).astype(jnp.bfloat16)


def product(a, b, dims):
    a_hi, a_lo = split(a)
    b_hi, b_lo = split(b)
    value = lax.dot_general(a_hi, b_hi, dims, preferred_element_type=jnp.float32)
    value += lax.dot_general(a_hi, b_lo, dims, preferred_element_type=jnp.float32)
    return value + lax.dot_general(a_lo, b_hi, dims, preferred_element_type=jnp.float32)


def kernel(
    nz, ny,
    *refs,
):
    given, (out, count_s), held = refs[:10], refs[10:12], refs[12:22]
    round_s, irr_s, pair_s, screen_s, order_s, irr_v, coup, amps, lad, cyc = held
    (
        psub, pan, lhs, lhs_hi, lhs_lo, pack, place, part, xs, xb, ys, yb, res4, full, own, send, back,
        sem_in, sem_a, sem_b, sem_c, sem_x, sem_y, sem_f, sem_h,
    ) = refs[22:]
    nblk = 4 * nz
    occ = amps.shape[1]
    slots = ROWS * CAP
    g = lax.axis_index("grp")
    b = lax.axis_index("blk")
    z = lax.div(b, 4)
    plane = lax.rem(b, 4)
    h = lax.div(plane, 2)
    c = lax.rem(plane, 2)
    y = lax.div(g, 2)
    xl = lax.rem(g, 2)
    x_dev = z * 4 + (1 - h) * 2 + c
    c_dev = z * 4 + h * 2 + (1 - c)
    x_plane = (1 - h) * 2 + c

    barrier = pltpu.get_barrier_semaphore()

    def greet(where):
        pl.semaphore_signal(barrier, inc=1, device_id=where, device_id_type=pl.DeviceIdType.MESH)

    def z_dev(d):
        return {"blk": lax.rem(z + nz + d, nz) * 4 + plane}

    def y_dev(d):
        return {"grp": lax.rem(y + ny + d, ny) * 2 + xl}

    x_pair = {"grp": y * 2 + 1 - xl}
    for d in (1, -1):
        greet(z_dev(d))
        greet({"blk": lax.rem(z + nz + d, nz) * 4 + x_plane})
    for d in range(1, 4):
        greet({"blk": z * 4 + lax.rem(plane + d, 4)})
    greet(x_pair)
    for d in range(1, ny):
        greet(y_dev(d))

    def fetch(n):
        return pltpu.make_async_copy(given[n], held[n], sem_in.at[n])

    for n in (8, 9, 2, 3, 1, 4, 0, 5, 6, 7):
        fetch(n).start()
    for n in (2, 3, 8, 9):
        fetch(n).wait()

    my_label = pair_s[g]
    tile_id = lax.div(b, 2)
    same = jnp.where(pair_s[tile_id] == my_label, 1.0, 0.0)
    kept = same * screen_s[g, tile_id].astype(jnp.float32)
    lad_t = lad[...] * kept
    cyc_t = cyc[...] * same
    for s in range(2):
        psub[s, :, 0:TILE] = lad_t[32 * s : 32 * s + 32]
        psub[s, :, TILE : 2 * TILE] = cyc_t[32 * s : 32 * s + 32]
    pan[z, h] = psub[h]

    for n in (0, 1, 4, 5, 6, 7):
        fetch(n).wait()

    irr_b = jnp.broadcast_to(irr_v[...].astype(jnp.float32), (occ, occ))
    irr_t = irr_b.T
    equal = irr_b == irr_t
    before = lax.broadcasted_iota(jnp.int32, (occ, occ), 0) < lax.broadcasted_iota(
        jnp.int32, (occ, occ), 1
    )
    rank = jnp.sum(jnp.where(equal & before, 1.0, 0.0), axis=0, keepdims=True)
    key = irr_v[...].astype(jnp.float32) * occ + rank
    first_rank = (round_s[0] * CAP).astype(jnp.float32)

    def joint_of(label):
        lane = lax.broadcasted_iota(jnp.int32, (1, 4 * slots), 1)
        row_of, slot_of = lax.div(lane, CAP), lax.rem(lane, CAP).astype(jnp.float32)
        irr_f = irr_v[...].astype(jnp.float32)
        goal = jnp.full((1, 4 * slots), -1.0, jnp.float32)
        start = jnp.full((1, 1), 0.0, jnp.float32) - (round_s[1] * JOINT).astype(jnp.float32)
        for row in range(4 * ROWS):
            want = (irr_s[z * 4 * ROWS + row] ^ label).astype(jnp.float32)
            fits = (irr_f == want) & (rank >= first_rank) & (rank < first_rank + CAP)
            size = jnp.sum(jnp.where(fits, 1.0, 0.0), axis=1, keepdims=True)
            goal = jnp.where((row_of == row) & (slot_of < size), start + slot_of, goal)
            start = start + size
        at = lax.broadcasted_iota(jnp.int32, (JOINT, 4 * slots), 0).astype(jnp.float32)
        return jnp.where(at == jnp.broadcast_to(goal, at.shape), 1.0, 0.0).astype(jnp.bfloat16)

    def targets(label, place):
        goal = place.astype(jnp.float32)
        for i in reversed(range(ROWS)):
            base = (irr_s[b * ROWS + i] ^ label) * occ + round_s[0] * CAP - CAP * i
            at = place.astype(jnp.float32) + base.astype(jnp.float32)
            goal = at if i == ROWS - 1 else jnp.where(place < CAP * (i + 1), at, goal)
        return goal

    key_b = jnp.broadcast_to(key, (slots, occ))
    sel = jnp.where(
        key_b == targets(my_label, lax.broadcasted_iota(jnp.int32, (slots, occ), 0)), 1.0, 0.0
    )
    coupling = jnp.where(equal, coup[...], 0.0)
    sel_c = product(sel, coupling, NT)
    for i in range(ROWS):
        rows = slice(CAP * i, CAP * i + CAP)
        pick = jnp.concatenate((sel[rows], sel_c[rows]), axis=0)
        packed = product(pick, amps[i], NN)
        lhs[plane, rows, 0:TILE] = packed[:CAP]
        lhs[plane, rows, TILE : 2 * TILE] = packed[CAP:]

    pl.semaphore_wait(barrier, 8 + ny - 1)

    def remote(src, dst, sems, index, where):
        return pltpu.make_async_remote_copy(
            src_ref=src,
            dst_ref=dst,
            send_sem=sems.at[(0, *index)],
            recv_sem=sems.at[(1, *index)],
            device_id=where,
            device_id_type=pl.DeviceIdType.MESH,
        )

    def to_x():
        return remote(psub.at[1 - h], pan.at[z, h], sem_b, (0,), {"blk": x_dev})

    def from_x():
        return remote(psub.at[1 - h], pan.at[z, 1 - h], sem_b, (0,), {"blk": x_dev})

    def to_x_z(way):
        step = 1 - 2 * way
        return remote(
            psub.at[1 - h], pan.at[z, h], sem_c, (1, way, 1),
            {"blk": lax.rem(z + nz + step, nz) * 4 + x_plane},
        )

    tiles = (h, 1 - h)
    reach = ((nz // 2, nz - 1 - nz // 2), (nz - 1 - nz // 2, nz // 2))

    def pass_z(kind, way, t):
        step = 1 - 2 * way
        src = lax.rem(z + nz - step * (t - 1), nz)
        at = pan.at[src, tiles[kind]]
        return remote(at, at, sem_c, (kind, way, t), z_dev(step))

    def got_z(kind, way, t):
        step = 1 - 2 * way
        src = lax.rem(z + nz - step * t, nz)
        at = pan.at[src, tiles[kind]]
        return remote(at, at, sem_c, (kind, way, t), z_dev(step))

    def start_z(kind, t):
        for way in range(2):
            if t <= reach[kind][way]:
                if t > 1:
                    got_z(kind, way, t - 1).wait_recv()
                pass_z(kind, way, t).start()

    def rows_to(src, where, k):
        return remote(lhs.at[src], lhs.at[src], sem_a, (k,), {"blk": where})

    to_x().start()
    for way in range(2):
        if reach[1][way]:
            to_x_z(way).start()
    start_z(0, 1)
    rows_to(plane, x_dev, 0).start()
    rows_to(plane, c_dev, 1).start()
    for kind in range(2):
        start_z(kind, 2)
    pack[...] = joint_of(my_label)
    for kind in range(2):
        start_z(kind, 3)
    from_x().wait_recv()
    rows_to(x_plane, x_dev, 0).wait_recv()
    rows_to(x_plane, c_dev, 2).start()
    for kind in range(2):
        for t in range(4, nz // 2 + 1):
            start_z(kind, t)
    rows_to(h * 2 + 1 - c, c_dev, 1).wait_recv()
    rows_to((1 - h) * 2 + 1 - c, c_dev, 2).wait_recv()
    hi, lo = split(lhs[...].reshape(4 * slots, 2 * TILE))
    lhs_hi[...] = jnp.dot(pack[...], hi, preferred_element_type=jnp.float32).astype(jnp.bfloat16)
    lhs_lo[...] = jnp.dot(pack[...], lo, preferred_element_type=jnp.float32).astype(jnp.bfloat16)

    def multiply(src):
        hi, lo = split(pan[src].reshape(64, 2 * TILE))
        value = lax.dot_general(hi, lhs_hi[...], NT, preferred_element_type=jnp.float32)
        value += lax.dot_general(hi, lhs_lo[...], NT, preferred_element_type=jnp.float32)
        value += lax.dot_general(lo, lhs_hi[...], NT, preferred_element_type=jnp.float32)
        part[src * 2] = value[:32]
        part[src * 2 + 1] = value[32:]

    multiply(z)
    for t in range(1, nz // 2 + 1):
        for way in range(2):
            for kind in range(2):
                if t == reach[kind][way]:
                    got_z(kind, way, t).wait_recv()
        multiply(lax.rem(z + nz - t, nz))
        if 2 * t < nz:
            multiply(lax.rem(z + t, nz))

    def pair_copy(k):
        return remote(xs.at[k], xb.at[k], sem_x, (k,), x_pair)

    def y_copy(k):
        return remote(ys.at[k], yb.at[k], sem_y, (k,), y_dev(k))

    def owner(k):
        return lax.rem(y + k, ny) * 2

    order = []
    for far in range(ny // 2, 0, -1):
        order += [far] if 2 * far == ny else [far, ny - far]
    for k in order + [0]:
        xs[k] = part[order_s[owner(k) + 1 - xl]]
        pair_copy(k).start()
    for k in order:
        pair_copy(k).wait_recv()
        ys[k] = part[order_s[owner(k) + xl]] + xb[k]
        y_copy(k).start()
    out_label = pair_s[order_s[g]]
    pack[...] = joint_of(out_label)
    key_t = jnp.broadcast_to(key, (slots, occ)).T
    lane = lax.broadcasted_iota(jnp.int32, (occ, slots), 1)
    where = key_t == targets(out_label, lane)
    for i in range(ROWS):
        mine = where & (lane >= CAP * i) & (lane < CAP * (i + 1))
        place[occ * i : occ * (i + 1)] = jnp.where(mine, 1.0, 0.0).astype(jnp.bfloat16)
    pair_copy(0).wait_recv()
    total = part[order_s[g]] + xb[0]
    for k in order:
        y_copy(k).wait_recv()
        total += yb[k]
    hi, lo = split(total)
    total = jnp.dot(hi, pack[...], preferred_element_type=jnp.float32)
    total += jnp.dot(lo, pack[...], preferred_element_type=jnp.float32)

    quarter = c * 2 + h
    for r in range(4):
        res4[r] = total[:, slots * r : slots * (r + 1)]

    def plane_copy(d):
        to = lax.rem(plane + d, 4)
        return remote(res4.at[to], full.at[quarter], sem_f, (d,), {"blk": z * 4 + to})

    for d in range(1, 4):
        plane_copy(d).start()
    full[quarter] = res4[plane]

    for d in range(1, 4):
        other = lax.rem(plane + 4 - d, 4)
        other_quarter = lax.rem(other, 2) * 2 + lax.div(other, 2)
        remote(res4.at[0], full.at[other_quarter], sem_f, (d,), {"blk": c_dev}).wait_recv()
    hi, lo = split(full[...].reshape(TILE, slots).T)
    value = jnp.dot(place[...], hi, preferred_element_type=jnp.float32)
    value += jnp.dot(place[...], lo, preferred_element_type=jnp.float32)
    for i in range(ROWS):
        own[i] = value[occ * i : occ * (i + 1)]
        send[pl.ds(i, occ, stride=ROWS), :] = value[occ * i : occ * (i + 1)]

    def swap(d):
        to = lax.rem(b + d, nblk)
        return remote(
            send.at[pl.ds(pl.multiple_of(to * 16, 16), 16)],
            back.at[pl.ds(pl.multiple_of(b * 16, 16), 16)],
            sem_h,
            (0,),
            {"blk": to},
        )

    def all_swaps():
        most = pl.ds(0, 16 * (nblk - 1))
        return remote(send.at[most], back.at[most], sem_h, (0,), {"blk": c_dev})

    def start_swap(m, carry):
        n = nblk - m
        odd = lax.rem(n, 2)
        half = lax.div(n, 2)
        swap(odd * (half + 1) + (1 - odd) * (nblk - half)).start()
        return carry

    lax.fori_loop(1, nblk, start_swap, 0)
    here = pl.ds(pl.multiple_of(b * 16, 16), 16)
    back[here] = send[here]

    irr_bi = irr_b.astype(jnp.int32)
    irr_ti = irr_t.astype(jnp.int32)
    plane_of = lax.broadcasted_iota(jnp.int32, (8, occ), 0) == lax.div(
        lax.broadcasted_iota(jnp.int32, (8, occ), 1), 4 * ROWS
    )
    plane_of = jnp.where(plane_of, 1.0, 0.0)
    worst = jnp.zeros((8, occ), jnp.float32)
    for label in range(8):
        hit = ((irr_bi ^ irr_ti) == label) & (rank < CAP)
        filled = jnp.dot(
            plane_of.astype(jnp.bfloat16),
            jnp.where(hit, 1.0, 0.0).astype(jnp.bfloat16),
            preferred_element_type=jnp.float32,
        )
        worst = jnp.maximum(worst, jnp.sum(filled, axis=1, keepdims=True))
    chunks = lax.div(jnp.max(worst).astype(jnp.int32) + JOINT - 1, JOINT)
    count_s[0] = lax.div(jnp.max(rank).astype(jnp.int32) + CAP, CAP) * chunks
    count_s[1] = chunks

    to_x().wait_send()
    rows_to(plane, x_dev, 0).wait_send()
    rows_to(plane, c_dev, 1).wait_send()
    rows_to(x_plane, c_dev, 2).wait_send()

    for kind in range(2):
        for way in range(2):
            for t in range(1, reach[kind][way] + 1):
                (to_x_z(way) if (kind, t) == (1, 1) else pass_z(kind, way, t)).wait_send()
    for k in order + [0]:
        pair_copy(k).wait_send()
    for k in order:
        y_copy(k).wait_send()
    for d in range(1, 4):
        plane_copy(d).wait_send()
    all_swaps().wait_recv()
    for j in range(ROWS):
        for i in range(ROWS):
            at = pl.ds(i, nblk, stride=ROWS)
            out[j, at, :] = own[j, at, :] - back[pl.ds(ROWS * j + i, nblk, stride=16), :]

    all_swaps().wait_send()


def shards(
    amplitudes, ladder_ints, cycle_ints, occ_coupling, occ_irrep, pair_irrep, screen, block_order
):
    rows, occ, tile = amplitudes.shape
    nz = lax.axis_size("blk") // 4
    ny = lax.axis_size("grp") // 2
    slots = ROWS * CAP
    f32 = jnp.float32
    smem = pl.BlockSpec(memory_space=pltpu.SMEM)
    vmem = pl.BlockSpec(memory_space=pltpu.VMEM)
    dma = pltpu.SemaphoreType.DMA
    call = pl.pallas_call(
        functools.partial(kernel, nz, ny),
        out_shape=(
            jax.ShapeDtypeStruct((rows, occ, tile), f32),
            jax.ShapeDtypeStruct((2,), jnp.int32),
        ),
        in_specs=[pl.BlockSpec(memory_space=pltpu.HBM)] * 10,
        out_specs=(vmem, smem),
        scratch_shapes=[
            pltpu.SMEM((3,), jnp.int32),
            pltpu.SMEM(occ_irrep.shape, jnp.int32),
            pltpu.SMEM(pair_irrep.shape, jnp.int32),
            pltpu.SMEM(screen.shape, jnp.int32),
            pltpu.SMEM(block_order.shape, jnp.int32),
            pltpu.VMEM((1, occ), jnp.int32),
            pltpu.VMEM((occ, occ), f32),
            pltpu.VMEM((rows, occ, tile), f32),
            pltpu.VMEM(ladder_ints.shape[::-1], f32),
            pltpu.VMEM(cycle_ints.shape[::-1], f32),
            pltpu.VMEM((2, 32, 2 * TILE), f32),
            pltpu.VMEM((nz, 2, 32, 2 * TILE), f32),
            pltpu.VMEM((4, slots, 2 * TILE), f32),
            pltpu.VMEM((JOINT, 2 * TILE), jnp.bfloat16),
            pltpu.VMEM((JOINT, 2 * TILE), jnp.bfloat16),
            pltpu.VMEM((JOINT, 4 * slots), jnp.bfloat16),
            pltpu.VMEM((rows * occ, slots), jnp.bfloat16),
            pltpu.VMEM((2 * nz, 32, JOINT), f32),
            pltpu.VMEM((ny, 32, JOINT), f32),
            pltpu.VMEM((ny, 32, JOINT), f32),
            pltpu.VMEM((ny, 32, JOINT), f32),
            pltpu.VMEM((ny, 32, JOINT), f32),
            pltpu.VMEM((4, 32, slots), f32),
            pltpu.VMEM((4, 32, slots), f32),
            pltpu.VMEM((rows, occ, tile), f32),
            pltpu.VMEM((rows * occ, tile), f32),
            pltpu.VMEM((rows * occ, tile), f32),
            dma((10,)),
            dma((2, 3)),
            dma((2, 1)),
            dma((2, 2, 2, nz // 2 + 1)),
            dma((2, ny)),
            dma((2, ny)),
            dma((2, 4)),
            dma((2, 1)),
        ],
        compiler_params=pltpu.CompilerParams(
            collective_id=0, has_side_effects=True, vmem_limit_bytes=24 << 20
        ),
    )

    def part(index):
        return call(
            index,
            occ_irrep, pair_irrep, screen, block_order, occ_irrep.reshape(1, occ),
            occ_coupling, amplitudes, ladder_ints.T, cycle_ints.T,
        )

    first, count = part(np.array((0, 0, 1), np.int32))

    def more(state):
        return state[0] < count[0]

    def again(state):
        index = jnp.stack((lax.div(state[0], count[1]), lax.rem(state[0], count[1]), jnp.int32(1)))
        return state[0] + 1, state[1] + part(index)[0]

    def rest(value):
        return lax.while_loop(more, again, (jnp.int32(1), value))[1]

    return lax.cond(count[0] > 1, rest, lambda value: value, first)


def solution(mesh):
    placed = (P("blk", None, "grp"), P("grp", "blk"), P("grp", "blk"), P(), P(), P(), P(), P())
    return jax.shard_map(
        shards, mesh=mesh, in_specs=placed, out_specs=P("blk", None, "grp"), check_vma=False
    )
```
